256 devices in a mesh: blk: 16 (over z_lo, x), tm: 16 (over y, z_hi, core).
Axes of the slice: x: 4, y: 4, z: 8 (z_hi: 2, z_lo: 4; z = z_hi * 4 + z_lo), core: 2. Of those that a mesh axis runs over, the one named last changes fastest.
Arguments:
- intensity: bfloat16 [3072, 32768], P('tm', 'blk'), may hold values from 0.04 to 330, as said below
- block_cycle: int32 [256], P('blk'), may hold values from 0 to 15, as said below
- cycle_order: int32 [16], replicated, may hold values from 0 to 15, as said below
Outputs:
- twotime: float32 [16, 3072, 3072], P('blk', 'tm')
The draws below stay inside these ranges and needn't reach their ends.
Inputs may be any that keep to these rules, and one draw needn't show every extreme that they name: `intensity`: positive corrected intensities. `block_cycle`: every cycle holds 1 to 31 blocks of the whole detector, and some cycle exactly 31; the 16 blocks of one index of blk hold at most 2 blocks of one cycle, and exactly 2 for some cycle. `cycle_order`: each cycle once.
All inputs are finite; a program needn't handle non-finite values.
Results may differ from the reference program's by a relative error of at most 0.0003.
Values may be sent and summed in bfloat16 or wider, within the bound.
A program may use at most 64 MiB of HBM per device.

```python
import math
import jax
import jax.numpy as jnp
from jax import lax

BLOCK = 128
BLK_DEV = 16
PANEL = 192
CAP = 2
CYCLES = 16
RCAP = 31
NBLK = 256
PIXELS = 32768
FRAMES = 3072


def draw_intensity(key, part):
    keys = jax.random.split(jax.random.fold_in(key, 7), 3)
    base = jnp.exp(jax.random.uniform(keys[0], (FRAMES, PIXELS), jnp.float32, math.log(0.05), math.log(2.0)))
    frame_scale = jnp.exp(jax.random.uniform(keys[1], (FRAMES, 1), jnp.float32, 0.0, math.log(10.0)))
    pixel_scale = jnp.exp(jax.random.uniform(keys[2], (1, PIXELS), jnp.float32, 0.0, math.log(10.0)))
    return (base * frame_scale * pixel_scale).astype(jnp.bfloat16)


def cycle_plan(key):
    half = CYCLES // 2
    keys = jax.random.split(jax.random.fold_in(key, 3), 5)
    spread = jax.random.randint(keys[0], (half,), 0, BLK_DEV).astype(jnp.int32)
    spread = spread.at[0].set(BLK_DEV - 1)
    sizes = jnp.concatenate([BLK_DEV + spread, BLK_DEV - spread]).astype(jnp.int32)
    labels = jax.random.permutation(keys[1], CYCLES).astype(jnp.int32)
    order = jax.random.permutation(keys[2], CYCLES).astype(jnp.int32)
    run_sizes = sizes[order]
    run_labels = labels[order]
    ends = jnp.cumsum(run_sizes).astype(jnp.int32)
    offset = jax.random.randint(keys[3], (), 0, NBLK).astype(jnp.int32)
    position = jnp.arange(NBLK, dtype=jnp.int32)
    shifted = (position + offset) % NBLK
    run = jnp.sum((shifted[:, None] >= ends[None, :]).astype(jnp.int32), axis=1)
    cycle_here = run_labels[run]
    device = position // CAP % CYCLES
    local = position // (CAP * CYCLES) * CAP + position % CAP
    block = device * BLK_DEV + local
    block_cycle = jnp.zeros((NBLK,), jnp.int32).at[block].set(cycle_here)
    biggest = labels[0]
    first_block = jnp.min(jnp.where(block_cycle == biggest, position, NBLK)).astype(jnp.int32)
    target = (first_block // BLK_DEV + half) % CYCLES
    perm = jax.random.permutation(keys[4], CYCLES).astype(jnp.int32)
    cycle_ids = jnp.arange(CYCLES, dtype=jnp.int32)
    where_big = jnp.sum(jnp.where(perm == biggest, cycle_ids, 0)).astype(jnp.int32)
    displaced = perm[target]
    perm = perm.at[where_big].set(displaced)
    perm = perm.at[target].set(biggest)
    return (block_cycle, perm)


def draw_block_cycle(key, part):
    return cycle_plan(key)[0]


def draw_cycle_order(key, part):
    return cycle_plan(key)[1]


def setup_inputs(seed: int = 0) -> dict:
    key_of = jax.random.split(jax.random.key(seed), 4)
    intensity = draw_intensity(jax.random.fold_in(key_of[3], 71), 0)
    block_cycle = draw_block_cycle(jax.random.fold_in(key_of[3], 71), 0)
    cycle_order = draw_cycle_order(jax.random.fold_in(key_of[3], 71), 0)
    return dict(intensity=intensity, block_cycle=block_cycle, cycle_order=cycle_order)


def reference(intensity, block_cycle, cycle_order):
    blocks = intensity.reshape(FRAMES, NBLK, BLOCK)
    tile_of = jnp.arange(FRAMES, dtype=jnp.int32) // PANEL
    upper = tile_of[:, None] <= tile_of[None, :]

    def one_cycle(cycle):
        member = block_cycle == cycle
        keyed = jnp.where(member, 0, 1).astype(jnp.int32)
        picked = jnp.argsort(keyed, stable=True)[:RCAP].astype(jnp.int32)
        valid = member[picked].astype(jnp.float32)
        rows = jnp.take(blocks, picked, axis=1).astype(jnp.float32) * valid[None, :, None]
        rows = rows.reshape(FRAMES, RCAP * BLOCK)
        gram = jnp.dot(rows, rows.T, precision=lax.Precision.HIGHEST)
        sums = jnp.sum(rows, axis=1)
        count = jnp.sum(member.astype(jnp.float32)) * BLOCK
        scaled = gram * count / (sums[:, None] * sums[None, :])
        return jnp.where(upper, scaled, jnp.float32(0.0))

    return lax.map(one_cycle, cycle_order)
```

```python
import functools

import jax
import jax.numpy as jnp
from jax import lax
from jax.experimental import pallas as pl
from jax.experimental.pallas import tpu as pltpu
from jax.sharding import PartitionSpec as P

BLOCK = 128
MESH = pl.DeviceIdType.MESH
NY = 4
W = 2 * BLOCK


def prep_kernel(bc_ref, order_ref, x_ref, o_ref):
    blk_dev = x_ref.shape[1] // BLOCK

    def one(s, carry):
        cyc = order_ref[s]
        first = jnp.int32(-1)
        second = jnp.int32(-1)
        for j in range(blk_dev):
            hit = bc_ref[j] == cyc
            second = jnp.where(jnp.logical_and(hit, first >= 0), j, second)
            first = jnp.where(jnp.logical_and(hit, first < 0), j, first)
        for r, src in ((0, first), (1, second)):
            cols = pl.ds(r * BLOCK, BLOCK)

            @pl.when(src >= 0)
            def _():
                start = pl.multiple_of(src * BLOCK, BLOCK)
                o_ref[s, :, cols] = x_ref[:, pl.ds(start, BLOCK)]

            @pl.when(src < 0)
            def _():
                o_ref[s, :, cols] = jnp.zeros((x_ref.shape[0], BLOCK), x_ref.dtype)

        return carry

    lax.fori_loop(0, order_ref.shape[0], one, 0)


def dot_t(a, b):
    return lax.dot_general(a, b, (((1,), (1,)), ((), ())), preferred_element_type=jnp.float32)


def main_kernel(
    out_ref, gram_ref, s_ref,
    a_buf, o_buf, cs, cx, rs, rx, tsum, ret,
    st_send, st_recv, y_send, y_recv, c_send, c_recv, t_send, t_recv, s_send, s_recv,
):
    nblk, panel, _ = out_ref.shape
    nsrc = nblk // 2
    b = lax.axis_index("blk")
    t = lax.axis_index("tm")
    c = t % 2
    h = (t // 2) % 2
    y = t // 4
    bp = b % 2
    bm = b // 2
    half = 2 * panel

    def tm_of(yy, hh, cc):
        return (yy * 2 + hh) * 2 + cc

    other = (b, tm_of(y, h, 1 - c))

    barrier = pltpu.get_barrier_semaphore()

    def greet(k, carry):
        s = (b + k) % nblk
        for j in range(4):
            pl.semaphore_signal(barrier, inc=1, device_id=(s, y * 4 + j), device_id_type=MESH)
        return carry

    lax.fori_loop(1, nblk, greet, 0)
    for j in range(1, 4):
        pl.semaphore_signal(barrier, inc=1, device_id=(b, y * 4 + (t + j) % 4), device_id_type=MESH)
    for r in range(1, NY):
        for q in range(2):
            pl.semaphore_signal(
                barrier, inc=1, device_id=(b, tm_of((y + r) % NY, h, q)), device_id_type=MESH
            )
    pl.semaphore_wait(barrier, (nblk - 1) * 4 + 3 + (NY - 1) * 2)

    my_rows = pl.ds(pl.multiple_of(c * panel, panel), panel)
    my_cols = pl.ds(pl.multiple_of(bm * W, W), W)

    def st_copy(k, d):
        s = (b + k) % nblk
        dst = a_buf.at[y, my_rows, my_cols] if d == 0 else o_buf.at[my_rows, my_cols]
        return pltpu.make_async_remote_copy(
            src_ref=out_ref.at[s],
            dst_ref=dst,
            send_sem=st_send.at[d, k],
            recv_sem=st_recv.at[d, bm, c],
            device_id=(s, tm_of(y, h if d == 0 else 1 - h, bp)),
            device_id_type=MESH,
        )

    def local_copy():
        return pltpu.make_async_copy(
            out_ref.at[b], a_buf.at[y, my_rows, my_cols], st_recv.at[0, bm, c]
        )

    st_copy(0, 1).start()

    @pl.when(bp == c)
    def _():
        local_copy().start()

    @pl.when(bp != c)
    def _():
        st_copy(0, 0).start()

    def send_one(k, carry):
        for d in range(2):
            st_copy(k, d).start()
        return carry

    lax.fori_loop(1, nblk, send_one, 0)

    def st_wait(d, m, q):
        rows = pl.ds(q * panel, panel)
        cols = pl.ds(pl.multiple_of(m * W, W), W)
        dst = a_buf.at[y, rows, cols] if d == 0 else o_buf.at[rows, cols]
        pltpu.make_async_remote_copy(
            src_ref=out_ref.at[0], dst_ref=dst, send_sem=st_send.at[d, 0], recv_sem=st_recv.at[d, m, q],
            device_id=other, device_id_type=MESH,
        ).wait_recv()

    def y_copy(m, r, src_y, to_y):
        cols = pl.ds(pl.multiple_of(m * W, W), W)
        return pltpu.make_async_remote_copy(
            src_ref=a_buf.at[src_y, :, cols],
            dst_ref=a_buf.at[src_y, :, cols],
            send_sem=y_send.at[m, r],
            recv_sem=y_recv.at[m, r],
            device_id=(b, tm_of(to_y, h, c)),
            device_id_type=MESH,
        )

    def forward(m, carry):
        for q in range(2):
            st_wait(0, m, q)
        for r in range(1, NY):
            y_copy(m, r, y, (y + r) % NY).start()
        return carry

    lax.fori_loop(0, nsrc, forward, 0)

    def wait_other(m, carry):
        for q in range(2):
            st_wait(1, m, q)
        return carry

    lax.fori_loop(0, nsrc, wait_other, 0)

    ones = jnp.ones((8, nsrc * W), jnp.bfloat16)
    own_sum = dot_t(ones, a_buf[y])
    oth_sum = dot_t(ones, o_buf[...])
    head = a_buf[y, 0:16, :].astype(jnp.float32)
    lane = lax.broadcasted_iota(jnp.int32, head.shape, 1)
    row = lax.broadcasted_iota(jnp.int32, head.shape, 0)
    mark = jnp.where(jnp.logical_and(lane % BLOCK == 0, row == 0), head, 0.0)
    filled = jnp.sum(jnp.where(mark > 0.0, 1.0, 0.0))
    srow = lax.broadcasted_iota(jnp.int32, (8, half), 0)
    s_ref[c, y, :, pl.ds(pl.multiple_of(h * half, half), half)] = jnp.where(srow == 1, filled, own_sum)
    s_ref[c, y, :, pl.ds(pl.multiple_of((1 - h) * half, half), half)] = jnp.where(srow == 1, filled, oth_sum)

    def s_copy(r, q, cc, yy, to):
        return pltpu.make_async_remote_copy(
            src_ref=s_ref.at[cc, yy], dst_ref=s_ref.at[cc, yy],
            send_sem=s_send.at[r, q], recv_sem=s_recv.at[r, q],
            device_id=to, device_id_type=MESH,
        )

    for r in range(NY):
        for q in range(2):
            if r == 0 and q == 0:
                continue
            cc = c if q == 0 else 1 - c
            s_copy(r, q, c, y, (b, tm_of((y + r) % NY, h, cc))).start()

    def wait_y(m, carry):
        for r in range(1, NY):
            y_copy(m, r, (y - r + NY) % NY, y).wait_recv()
        return carry

    lax.fori_loop(0, nsrc, wait_y, 0)

    theirs = pl.ds(pl.multiple_of((1 - c) * panel, panel), panel)
    mine = pl.ds(pl.multiple_of(c * panel, panel), panel)

    def c_copy(kind, u):
        src, dst = (cs, rs) if kind == 0 else (cx, rx)
        return pltpu.make_async_remote_copy(
            src_ref=src.at[u, theirs, :], dst_ref=dst.at[u],
            send_sem=c_send.at[kind, u], recv_sem=c_recv.at[kind, u],
            device_id=other, device_id_type=MESH,
        )

    def t_copy(yy, u):
        return pltpu.make_async_remote_copy(
            src_ref=tsum.at[u], dst_ref=ret.at[yy],
            send_sem=t_send.at[u], recv_sem=t_recv.at[yy],
            device_id=(b, tm_of(u, h, c)), device_id_type=MESH,
        )

    def cross(u, carry):
        @pl.when(u <= y)
        def _():
            cx[u] = dot_t(a_buf[u], o_buf[...])
            c_copy(1, u).start()
        return carry

    lax.fori_loop(0, NY, cross, 0)

    def same(u, carry):
        @pl.when(u >= y)
        def _():
            cs[u] = dot_t(a_buf[y], a_buf[u])
            c_copy(0, u).start()
        return carry

    lax.fori_loop(0, NY, same, 0)

    def combine(u, carry):
        @pl.when(u <= y)
        def _():
            c_copy(1, u).wait_recv()
            tsum[u] = cx[u, mine, :] + rx[u]

        @pl.when(u < y)
        def _():
            t_copy(y, u).start()
        return carry

    lax.fori_loop(0, NY, combine, 0)

    def place(u, carry):
        same_cols = pl.ds(pl.multiple_of(u * 2 * half + h * half, half), half)
        cross_cols = pl.ds(pl.multiple_of(u * 2 * half + (1 - h) * half, half), half)

        @pl.when(u < y)
        def _():
            gram_ref[:, same_cols] = jnp.zeros((panel, half), jnp.float32)
            gram_ref[:, cross_cols] = jnp.zeros((panel, half), jnp.float32)

        @pl.when(u >= y)
        def _():
            c_copy(0, u).wait_recv()
            gram_ref[:, same_cols] = cs[u, mine, :] + rs[u]

        @pl.when(u == y)
        def _():
            gram_ref[:, cross_cols] = tsum[u]

        @pl.when(u > y)
        def _():
            t_copy(u, y).wait_recv()
            gram_ref[:, cross_cols] = ret[u]
        return carry

    lax.fori_loop(0, NY, place, 0)

    for r in range(NY):
        for q in range(2):
            if r == 0 and q == 0:
                continue
            cc = c if q == 0 else 1 - c
            s_copy(r, q, cc, (y - r + NY) % NY, other).wait_recv()

    st_copy(0, 1).wait_send()

    @pl.when(bp != c)
    def _():
        st_copy(0, 0).wait_send()

    def drain_one(k, carry):
        for d in range(2):
            st_copy(k, d).wait_send()
        return carry

    lax.fori_loop(1, nblk, drain_one, 0)

    def drain_y(m, carry):
        for r in range(1, NY):
            y_copy(m, r, y, (y + r) % NY).wait_send()
        return carry

    lax.fori_loop(0, nsrc, drain_y, 0)

    def drain_c(u, carry):
        @pl.when(u <= y)
        def _():
            c_copy(1, u).wait_send()

        @pl.when(u >= y)
        def _():
            c_copy(0, u).wait_send()

        @pl.when(u < y)
        def _():
            t_copy(y, u).wait_send()
        return carry

    lax.fori_loop(0, NY, drain_c, 0)
    for r in range(NY):
        for q in range(2):
            if r == 0 and q == 0:
                continue
            s_copy(r, q, c, y, other).wait_send()


def on_device(intensity, block_cycle, cycle_order):
    panel = intensity.shape[0]
    nblk = cycle_order.shape[0]
    nsrc = nblk // 2
    half = 2 * panel
    frames = panel * lax.axis_size("tm")
    vmem = pl.BlockSpec(memory_space=pltpu.VMEM)
    smem = pl.BlockSpec(memory_space=pltpu.SMEM)
    outgoing = pl.pallas_call(
        prep_kernel,
        out_shape=jax.ShapeDtypeStruct((nblk, panel, W), jnp.bfloat16),
        in_specs=[smem, smem, vmem],
        out_specs=vmem,
        name="prep",
    )(block_cycle, cycle_order, intensity)
    dma = pltpu.SemaphoreType.DMA
    gram, parts = pl.pallas_call(
        main_kernel,
        out_shape=(
            jax.ShapeDtypeStruct((panel, frames), jnp.float32),
            jax.ShapeDtypeStruct((2, NY, 8, 2 * half), jnp.float32),
        ),
        in_specs=[vmem],
        out_specs=(vmem, vmem),
        scratch_shapes=[
            pltpu.VMEM((NY, half, nsrc * W), jnp.bfloat16),
            pltpu.VMEM((half, nsrc * W), jnp.bfloat16),
            pltpu.VMEM((NY, half, half), jnp.float32),
            pltpu.VMEM((NY, half, half), jnp.float32),
            pltpu.VMEM((NY, panel, half), jnp.float32),
            pltpu.VMEM((NY, panel, half), jnp.float32),
            pltpu.VMEM((NY, panel, half), jnp.float32),
            pltpu.VMEM((NY, panel, half), jnp.float32),
            dma((2, nblk)), dma((2, nsrc, 2)),
            dma((nsrc, NY)), dma((nsrc, NY)),
            dma((2, NY)), dma((2, NY)),
            dma((NY,)), dma((NY,)),
            dma((NY, 2)), dma((NY, 2)),
        ],
        compiler_params=pltpu.CompilerParams(
            collective_id=0, has_side_effects=True, vmem_limit_bytes=56 << 20
        ),
        name="exchange",
    )(outgoing)
    me = lax.axis_index("tm")
    y = me // 4
    sums = (parts[0, :, 0, :] + parts[1, :, 0, :]).reshape(frames)
    count = (parts[0, 0, 1, 0] + parts[1, 0, 1, 0]) * BLOCK
    own = lax.dynamic_slice(sums, (me * panel,), (panel,))
    column_panel = jnp.arange(frames, dtype=jnp.int32) // panel
    scaled = gram * count / (own[:, None] * sums[None, :])
    twotime = jnp.where((column_panel >= me)[None, :], scaled, jnp.float32(0.0))
    return twotime.reshape(1, panel, frames)


def solution(mesh):
    placed = (P("tm", "blk"), P("blk"), P())
    return jax.shard_map(
        on_device, mesh=mesh, in_specs=placed, out_specs=P("blk", "tm", None), check_vma=False
    )
```

```python
import jax
import jax.numpy as jnp
from jax import lax
from jax.experimental import pallas as pl
from jax.experimental.pallas import tpu as pltpu
from jax.sharding import PartitionSpec as P

BLOCK = 128
MESH = pl.DeviceIdType.MESH
NY = 4
W = 2 * BLOCK


def dot_t(a, b):
    return lax.dot_general(a, b, (((1,), (1,)), ((), ())), preferred_element_type=jnp.float32)


def main_kernel(
    bc_ref, order_ref, x_ref, out_ref,
    slots, a_buf, o_buf, acc_s, acc_x, rs, rx, tsum, sum_acc, s_mine, s_oth, s_tot, s_col,
    st_send, st_recv, y_send, y_recv, c_send, c_recv, t_send, t_recv, s_send, s_recv,
):
    nblk, panel, _ = slots.shape
    nsrc = nblk // 2
    b = lax.axis_index("blk")
    t = lax.axis_index("tm")
    c = t % 2
    h = (t // 2) % 2
    y = t // 4
    bp = b % 2
    bm = b // 2
    half = 2 * panel
    up = (y + 1) % NY
    down = (y + NY - 1) % NY
    far = (y + 2) % NY

    def tm_of(yy, hh, cc):
        return (yy * 2 + hh) * 2 + cc

    other = (b, tm_of(y, h, 1 - c))

    barrier = pltpu.get_barrier_semaphore()

    def greet(k, carry):
        s = (b + k) % nblk
        for j in range(4):
            pl.semaphore_signal(barrier, inc=1, device_id=(s, y * 4 + j), device_id_type=MESH)
        return carry

    lax.fori_loop(1, nblk, greet, 0)
    for j in range(1, 4):
        pl.semaphore_signal(barrier, inc=1, device_id=(b, y * 4 + (t + j) % 4), device_id_type=MESH)
    for r in range(1, NY):
        pl.semaphore_signal(
            barrier, inc=1, device_id=(b, tm_of((y + r) % NY, h, c)), device_id_type=MESH
        )

    blk_dev = x_ref.shape[1] // BLOCK

    def fill(s, carry):
        cyc = order_ref[s]
        first = jnp.int32(-1)
        second = jnp.int32(-1)
        for j in range(blk_dev):
            hit = bc_ref[j] == cyc
            second = jnp.where(jnp.logical_and(hit, first >= 0), j, second)
            first = jnp.where(jnp.logical_and(hit, first < 0), j, first)
        for r, src in ((0, first), (1, second)):
            start = jnp.maximum(src, 0) * BLOCK
            keep = jnp.where(src >= 0, jnp.float32(1.0), jnp.float32(0.0))
            block = x_ref[:, pl.ds(start, BLOCK)].astype(jnp.float32) * keep
            slots[s, :, pl.ds(r * BLOCK, BLOCK)] = block.astype(jnp.bfloat16)
        return carry

    lax.fori_loop(0, nblk, fill, 0)

    def clear(u, carry):
        acc_s[u] = jnp.zeros((half, half), jnp.float32)
        acc_x[u] = jnp.zeros((half, half), jnp.float32)
        return carry

    lax.fori_loop(0, NY, clear, 0)
    sum_acc[...] = jnp.zeros(sum_acc.shape, jnp.float32)

    pl.semaphore_wait(barrier, (nblk - 1) * 4 + 3 + (NY - 1))

    my_rows = pl.ds(pl.multiple_of(c * panel, panel), panel)
    my_cols = pl.ds(pl.multiple_of(bm * W, W), W)

    def st_copy(k, d):
        s = (b + k) % nblk
        dst = a_buf.at[y, my_rows, my_cols] if d == 0 else o_buf.at[my_rows, my_cols]
        return pltpu.make_async_remote_copy(
            src_ref=slots.at[s],
            dst_ref=dst,
            send_sem=st_send.at[d, k],
            recv_sem=st_recv.at[d, bm, c],
            device_id=(s, tm_of(y, h if d == 0 else 1 - h, bp)),
            device_id_type=MESH,
        )

    st_copy(0, 1).start()

    @pl.when(bp == c)
    def _():
        pltpu.make_async_copy(
            slots.at[b], a_buf.at[y, my_rows, my_cols], st_recv.at[0, bm, c]
        ).start()

    @pl.when(bp != c)
    def _():
        st_copy(0, 0).start()

    def send_one(k, carry):
        for d in range(2):
            st_copy(k, d).start()
        return carry

    lax.fori_loop(1, nblk, send_one, 0)

    def st_wait(d, m, q):
        rows = pl.ds(q * panel, panel)
        cols = pl.ds(pl.multiple_of(m * W, W), W)
        dst = a_buf.at[y, rows, cols] if d == 0 else o_buf.at[rows, cols]
        pltpu.make_async_remote_copy(
            src_ref=slots.at[0], dst_ref=dst, send_sem=st_send.at[d, 0], recv_sem=st_recv.at[d, m, q],
            device_id=other, device_id_type=MESH,
        ).wait_recv()

    whole = pl.ds(0, half)
    low = pl.ds(0, panel)
    high = pl.ds(panel, panel)

    def y_copy(m, way, src_y, rows, to_y):
        cols = pl.ds(pl.multiple_of(m * W, W), W)
        return pltpu.make_async_remote_copy(
            src_ref=a_buf.at[src_y, rows, cols],
            dst_ref=a_buf.at[src_y, rows, cols],
            send_sem=y_send.at[m, way],
            recv_sem=y_recv.at[m, way],
            device_id=(b, tm_of(to_y, h, c)),
            device_id_type=MESH,
        )

    def source(j):
        k = 2 * j + (b + c) % 2
        return ((b + nblk - k) % nblk) // 2

    ones = jnp.ones((8, W), jnp.bfloat16)

    def multiply(m):
        cols = pl.ds(pl.multiple_of(m * W, W), W)

        def job(u, carry):
            panel_u = a_buf[u, :, cols]
            sum_acc[u] += dot_t(ones, panel_u)

            @pl.when(u <= y)
            def _():
                acc_x[u] += dot_t(panel_u, o_buf[:, cols])

            @pl.when(u >= y)
            def _():
                acc_s[u] += dot_t(a_buf[y, :, cols], panel_u)
            return carry

        lax.fori_loop(0, NY, job, 0)
        sum_acc[NY] += dot_t(ones, o_buf[:, cols])

    def step(j, carry):
        @pl.when(j < nsrc)
        def _():
            m = source(j)
            for q in range(2):
                st_wait(0, m, q)
            y_copy(m, 0, y, whole, up).start()
            y_copy(m, 1, y, whole, down).start()

        @pl.when(jnp.logical_and(j >= 1, j < nsrc + 1))
        def _():
            m = source(j - 1)
            y_copy(m, 0, down, whole, y).wait_recv()
            y_copy(m, 2, down, low, up).start()
            y_copy(m, 1, up, whole, y).wait_recv()
            y_copy(m, 3, up, high, down).start()

        @pl.when(j >= 2)
        def _():
            m = source(j - 2)
            for q in range(2):
                st_wait(1, m, q)
            y_copy(m, 2, far, low, y).wait_recv()
            y_copy(m, 3, far, high, y).wait_recv()
            multiply(m)
        return carry

    lax.fori_loop(0, nsrc + 2, step, 0)

    theirs = pl.ds(pl.multiple_of((1 - c) * panel, panel), panel)
    mine = pl.ds(pl.multiple_of(c * panel, panel), panel)

    head = a_buf[y, 0:16, :].astype(jnp.float32)
    lane = lax.broadcasted_iota(jnp.int32, head.shape, 1)
    row = lax.broadcasted_iota(jnp.int32, head.shape, 0)
    mark = jnp.where(jnp.logical_and(lane % BLOCK == 0, row == 0), head, 0.0)
    filled = jnp.sum(jnp.where(mark > 0.0, 1.0, 0.0))
    srow = lax.broadcasted_iota(jnp.int32, sum_acc.shape, 1)
    s_mine[...] = jnp.where(srow == 1, filled, sum_acc[...])
    s_copy = pltpu.make_async_remote_copy(
        src_ref=s_mine, dst_ref=s_oth, send_sem=s_send, recv_sem=s_recv,
        device_id=other, device_id_type=MESH,
    )
    s_copy.start()

    def c_copy(kind, u):
        src, dst = (acc_s, rs) if kind == 0 else (acc_x, rx)
        return pltpu.make_async_remote_copy(
            src_ref=src.at[u, theirs, :], dst_ref=dst.at[u],
            send_sem=c_send.at[kind, u], recv_sem=c_recv.at[kind, u],
            device_id=other, device_id_type=MESH,
        )

    def t_copy(yy, u):
        cols = pl.ds(pl.multiple_of(yy * 2 * half + (1 - h) * half, half), half)
        return pltpu.make_async_remote_copy(
            src_ref=tsum.at[u], dst_ref=out_ref.at[:, cols],
            send_sem=t_send.at[u], recv_sem=t_recv.at[yy],
            device_id=(b, tm_of(u, h, c)), device_id_type=MESH,
        )

    def share_cross(u, carry):
        @pl.when(u <= y)
        def _():
            c_copy(1, u).start()
        return carry

    def share_same(u, carry):
        @pl.when(u >= y)
        def _():
            c_copy(0, u).start()
        return carry

    lax.fori_loop(0, NY, share_cross, 0)
    lax.fori_loop(0, NY, share_same, 0)

    s_copy.wait_recv()
    for u in range(NY + 1):
        total = s_mine[u] + s_oth[u]
        s_tot[u] = total
        s_col[u] = total.T
    count = s_tot[0, 1:2, 0:1] * BLOCK

    def scaled(g, u_row, u_col):
        si = s_col[u_row, mine, 0:1]
        sj = s_tot[u_col, 0:1, :]
        return g * count / (si * sj)

    def back(u, carry):
        @pl.when(u < y)
        def _():
            c_copy(1, u).wait_recv()
            tsum[u] = scaled(acc_x[u, mine, :] + rx[u], u, NY)
            t_copy(y, u).start()
        return carry

    lax.fori_loop(0, NY, back, 0)

    tile = lax.broadcasted_iota(jnp.int32, (panel, half), 1)

    def place(u, carry):
        same_cols = pl.ds(pl.multiple_of(u * 2 * half + h * half, half), half)
        cross_cols = pl.ds(pl.multiple_of(u * 2 * half + (1 - h) * half, half), half)

        @pl.when(u < y)
        def _():
            out_ref[:, same_cols] = jnp.zeros((panel, half), jnp.float32)
            out_ref[:, cross_cols] = jnp.zeros((panel, half), jnp.float32)

        @pl.when(u >= y)
        def _():
            c_copy(0, u).wait_recv()
            g = scaled(acc_s[u, mine, :] + rs[u], y, u)
            first_tile = u * 4 + h * 2
            tiles = first_tile + jnp.where(tile >= panel, 1, 0)
            out_ref[:, same_cols] = jnp.where(tiles >= t, g, 0.0)

        @pl.when(u == y)
        def _():
            c_copy(1, u).wait_recv()
            g = scaled(acc_x[u, mine, :] + rx[u], y, NY)
            first_tile = u * 4 + (1 - h) * 2
            tiles = first_tile + jnp.where(tile >= panel, 1, 0)
            out_ref[:, cross_cols] = jnp.where(tiles >= t, g, 0.0)
        return carry

    lax.fori_loop(0, NY, place, 0)

    def arrive(u, carry):
        @pl.when(u > y)
        def _():
            t_copy(u, y).wait_recv()
        return carry

    lax.fori_loop(0, NY, arrive, 0)

    st_copy(0, 1).wait_send()

    @pl.when(bp != c)
    def _():
        st_copy(0, 0).wait_send()

    def drain_one(k, carry):
        for d in range(2):
            st_copy(k, d).wait_send()
        return carry

    lax.fori_loop(1, nblk, drain_one, 0)

    def drain_y(m, carry):
        y_copy(m, 0, y, whole, up).wait_send()
        y_copy(m, 1, y, whole, down).wait_send()
        y_copy(m, 2, down, low, up).wait_send()
        y_copy(m, 3, up, high, down).wait_send()
        return carry

    lax.fori_loop(0, nsrc, drain_y, 0)

    def drain_c(u, carry):
        @pl.when(u <= y)
        def _():
            c_copy(1, u).wait_send()

        @pl.when(u >= y)
        def _():
            c_copy(0, u).wait_send()

        @pl.when(u < y)
        def _():
            t_copy(y, u).wait_send()
        return carry

    lax.fori_loop(0, NY, drain_c, 0)
    s_copy.wait_send()


def on_device(intensity, block_cycle, cycle_order):
    panel = intensity.shape[0]
    nblk = cycle_order.shape[0]
    nsrc = nblk // 2
    half = 2 * panel
    frames = panel * lax.axis_size("tm")
    vmem = pl.BlockSpec(memory_space=pltpu.VMEM)
    smem = pl.BlockSpec(memory_space=pltpu.SMEM)
    dma = pltpu.SemaphoreType.DMA
    twotime = pl.pallas_call(
        main_kernel,
        out_shape=jax.ShapeDtypeStruct((panel, frames), jnp.float32),
        in_specs=[smem, smem, vmem],
        out_specs=vmem,
        scratch_shapes=[
            pltpu.VMEM((nblk, panel, W), jnp.bfloat16),
            pltpu.VMEM((NY, half, nsrc * W), jnp.bfloat16),
            pltpu.VMEM((half, nsrc * W), jnp.bfloat16),
            pltpu.VMEM((NY, half, half), jnp.float32),
            pltpu.VMEM((NY, half, half), jnp.float32),
            pltpu.VMEM((NY, panel, half), jnp.float32),
            pltpu.VMEM((NY, panel, half), jnp.float32),
            pltpu.VMEM((NY, panel, half), jnp.float32),
            pltpu.VMEM((NY + 1, 8, half), jnp.float32),
            pltpu.VMEM((NY + 1, 8, half), jnp.float32),
            pltpu.VMEM((NY + 1, 8, half), jnp.float32),
            pltpu.VMEM((NY + 1, 8, half), jnp.float32),
            pltpu.VMEM((NY + 1, half, 8), jnp.float32),
            dma((2, nblk)), dma((2, nsrc, 2)),
            dma((nsrc, 4)), dma((nsrc, 4)),
            dma((2, NY)), dma((2, NY)),
            dma((NY,)), dma((NY,)),
            dma, dma,
        ],
        compiler_params=pltpu.CompilerParams(
            collective_id=0, has_side_effects=True, vmem_limit_bytes=56 << 20
        ),
        name="exchange",
    )(block_cycle, cycle_order, intensity)
    return twotime.reshape(1, panel, frames)


def solution(mesh):
    placed = (P("tm", "blk"), P("blk"), P())
    return jax.shard_map(
        on_device, mesh=mesh, in_specs=placed, out_specs=P("blk", "tm", None), check_vma=False
    )
```

```python
import jax
import jax.numpy as jnp
from jax import lax
from jax.experimental import pallas as pl
from jax.experimental.pallas import tpu as pltpu
from jax.sharding import PartitionSpec as P

BLOCK = 128
MESH = pl.DeviceIdType.MESH
NY = 4
W = 2 * BLOCK
STRIDE = 7
LAG = 1
AHEAD = 2
CUT = 2


def dot_t(a, b):
    return lax.dot_general(a, b, (((1,), (1,)), ((), ())), preferred_element_type=jnp.float32)


def main_kernel(
    bc_ref, order_ref, x_ref, out_ref,
    slots, a_buf, o_buf, acc_s, acc_x, rs, rx, tsum, sum_acc, s_mine, s_oth, s_tot, s_col,
    st_send, st_recv, y_send, y_recv, c_send, c_recv, t_send, t_recv, z_recv, s_send, s_recv,
):
    nblk, panel, _ = slots.shape
    nsrc = nblk // 2
    b = lax.axis_index("blk")
    t = lax.axis_index("tm")
    c = t % 2
    h = (t // 2) % 2
    y = t // 4
    bp = b % 2
    bm = b // 2
    half = 2 * panel
    up = (y + 1) % NY
    down = (y + NY - 1) % NY
    far = (y + 2) % NY

    def tm_of(yy, hh, cc):
        return (yy * 2 + hh) * 2 + cc

    other = (b, tm_of(y, h, 1 - c))

    barrier = pltpu.get_barrier_semaphore()

    def greet(k, carry):
        s = (b + k) % nblk
        for j in range(4):
            pl.semaphore_signal(barrier, inc=1, device_id=(s, y * 4 + j), device_id_type=MESH)
        return carry

    lax.fori_loop(1, nblk, greet, 0)
    for j in range(1, 4):
        pl.semaphore_signal(barrier, inc=1, device_id=(b, y * 4 + (t + j) % 4), device_id_type=MESH)
    for r in range(1, NY):
        pl.semaphore_signal(
            barrier, inc=1, device_id=(b, tm_of((y + r) % NY, h, c)), device_id_type=MESH
        )

    blk_dev = x_ref.shape[1] // BLOCK

    def target(i):
        return (b + i * STRIDE) % nblk

    def fill(i, carry):
        s = target(i)
        cyc = order_ref[s]
        first = jnp.int32(-1)
        second = jnp.int32(-1)
        for j in range(blk_dev):
            hit = bc_ref[j] == cyc
            second = jnp.where(jnp.logical_and(hit, first >= 0), j, second)
            first = jnp.where(jnp.logical_and(hit, first < 0), j, first)
        for r, src in ((0, first), (1, second)):
            start = jnp.maximum(src, 0) * BLOCK
            keep = jnp.where(src >= 0, jnp.float32(1.0), jnp.float32(0.0))
            block = x_ref[:, pl.ds(start, BLOCK)].astype(jnp.float32) * keep
            slots[s, :, pl.ds(r * BLOCK, BLOCK)] = block.astype(jnp.bfloat16)
        return carry

    lax.fori_loop(0, AHEAD, fill, 0)

    pl.semaphore_wait(barrier, (nblk - 1) * 4 + 3 + (NY - 1))

    my_rows = pl.ds(pl.multiple_of(c * panel, panel), panel)
    my_cols = pl.ds(pl.multiple_of(bm * W, W), W)

    def st_copy(i, d):
        s = target(i)
        dst = a_buf.at[y, my_rows, my_cols] if d == 0 else o_buf.at[my_rows, my_cols]
        return pltpu.make_async_remote_copy(
            src_ref=slots.at[s],
            dst_ref=dst,
            send_sem=st_send.at[d, i],
            recv_sem=st_recv.at[d, bm, c],
            device_id=(s, tm_of(y, h if d == 0 else 1 - h, bp)),
            device_id_type=MESH,
        )

    @pl.when(bp == c)
    def _():
        pltpu.make_async_copy(
            slots.at[b], a_buf.at[y, my_rows, my_cols], st_recv.at[0, bm, c]
        ).start()

    @pl.when(bp != c)
    def _():
        st_copy(0, 0).start()

    def send_one(i, carry):
        @pl.when(i + AHEAD - 1 < nblk)
        def _():
            fill(i + AHEAD - 1, 0)

        @pl.when(i < nblk)
        def _():
            st_copy(i, 0).start()

        @pl.when(i >= LAG)
        def _():
            st_copy(i - LAG, 1).start()
        return carry

    lax.fori_loop(1, nblk + LAG, send_one, 0)

    def clear(u, carry):
        acc_s[u] = jnp.zeros((half, half), jnp.float32)
        acc_x[u] = jnp.zeros((half, half), jnp.float32)
        return carry

    lax.fori_loop(0, NY, clear, 0)
    sum_acc[...] = jnp.zeros(sum_acc.shape, jnp.float32)

    def st_wait(d, m, q):
        rows = pl.ds(q * panel, panel)
        cols = pl.ds(pl.multiple_of(m * W, W), W)
        dst = a_buf.at[y, rows, cols] if d == 0 else o_buf.at[rows, cols]
        pltpu.make_async_remote_copy(
            src_ref=slots.at[0], dst_ref=dst, send_sem=st_send.at[d, 0], recv_sem=st_recv.at[d, m, q],
            device_id=other, device_id_type=MESH,
        ).wait_recv()

    whole = pl.ds(0, half)
    low = pl.ds(0, panel)
    high = pl.ds(panel, panel)

    def y_copy(m, way, src_y, rows, to_y):
        cols = pl.ds(pl.multiple_of(m * W, W), W)
        return pltpu.make_async_remote_copy(
            src_ref=a_buf.at[src_y, rows, cols],
            dst_ref=a_buf.at[src_y, rows, cols],
            send_sem=y_send.at[m, way],
            recv_sem=y_recv.at[m, way],
            device_id=(b, tm_of(to_y, h, c)),
            device_id_type=MESH,
        )

    def source(j):
        k = (2 * j + (b + c) % 2) * STRIDE % nblk
        return ((b + nblk - k) % nblk) // 2

    ones = jnp.ones((8, W), jnp.bfloat16)

    first = pl.ds(0, half - BLOCK)
    last = pl.ds(half - BLOCK, BLOCK)

    def split(u, v):
        return jnp.logical_and(u < CUT, v >= CUT)

    def near(u, v):
        return jnp.logical_and(u <= v, jnp.logical_or(u >= CUT, v < CUT))

    def multiply(m):
        cols = pl.ds(pl.multiple_of(m * W, W), W)

        def job(u, carry):
            panel_u = a_buf[u, :, cols]
            sum_acc[u] += dot_t(ones, panel_u)

            @pl.when(near(u, y))
            def _():
                acc_x[u] += dot_t(panel_u, o_buf[:, cols])

            @pl.when(split(u, y))
            def _():
                acc_x[u, :, first] += dot_t(panel_u, o_buf[first, cols])

            @pl.when(split(y, u))
            def _():
                acc_x[u, :, 0:BLOCK] += dot_t(o_buf[:, cols], a_buf[u, last, cols])

            @pl.when(u >= y)
            def _():
                acc_s[u] += dot_t(a_buf[y, :, cols], panel_u)
            return carry

        lax.fori_loop(0, NY, job, 0)
        sum_acc[NY] += dot_t(ones, o_buf[:, cols])

    def step(j, carry):
        @pl.when(j < nsrc)
        def _():
            m = source(j)
            for q in range(2):
                st_wait(0, m, q)
            y_copy(m, 0, y, whole, up).start()
            y_copy(m, 1, y, whole, down).start()

        @pl.when(jnp.logical_and(j >= 1, j < nsrc + 1))
        def _():
            m = source(j - 1)
            y_copy(m, 0, down, whole, y).wait_recv()
            y_copy(m, 2, down, low, up).start()
            y_copy(m, 1, up, whole, y).wait_recv()
            y_copy(m, 3, up, high, down).start()

        @pl.when(j >= 2)
        def _():
            m = source(j - 2)
            for q in range(2):
                st_wait(1, m, q)
            y_copy(m, 2, far, low, y).wait_recv()
            y_copy(m, 3, far, high, y).wait_recv()
            multiply(m)
        return carry

    lax.fori_loop(0, nsrc + 2, step, 0)

    theirs = pl.ds(pl.multiple_of((1 - c) * panel, panel), panel)
    mine = pl.ds(pl.multiple_of(c * panel, panel), panel)

    head = a_buf[y, 0:16, :].astype(jnp.float32)
    lane = lax.broadcasted_iota(jnp.int32, head.shape, 1)
    row = lax.broadcasted_iota(jnp.int32, head.shape, 0)
    mark = jnp.where(jnp.logical_and(lane % BLOCK == 0, row == 0), head, 0.0)
    filled = jnp.sum(jnp.where(mark > 0.0, 1.0, 0.0))
    srow = lax.broadcasted_iota(jnp.int32, sum_acc.shape, 1)
    s_mine[...] = jnp.where(srow == 1, filled, sum_acc[...])
    s_copy = pltpu.make_async_remote_copy(
        src_ref=s_mine, dst_ref=s_oth, send_sem=s_send, recv_sem=s_recv,
        device_id=other, device_id_type=MESH,
    )
    s_copy.start()

    def c_copy(kind, u):
        src, dst = (acc_s, rs) if kind == 0 else (acc_x, rx)
        return pltpu.make_async_remote_copy(
            src_ref=src.at[u, theirs, :], dst_ref=dst.at[u],
            send_sem=c_send.at[kind, u], recv_sem=c_recv.at[kind, u],
            device_id=other, device_id_type=MESH,
        )

    def t_copy(yy, u):
        cols = pl.ds(pl.multiple_of(yy * 2 * half + (1 - h) * half, half), half)
        return pltpu.make_async_remote_copy(
            src_ref=tsum.at[u], dst_ref=out_ref.at[:, cols],
            send_sem=t_send.at[u], recv_sem=t_recv.at[yy],
            device_id=(b, tm_of(u, h, c)), device_id_type=MESH,
        )

    def t_split(yy, u):
        start = yy * 2 * half + (1 - h) * half
        cols = pl.ds(pl.multiple_of(start, BLOCK), half - BLOCK)
        return pltpu.make_async_remote_copy(
            src_ref=tsum.at[u, :, first], dst_ref=out_ref.at[:, cols],
            send_sem=t_send.at[u], recv_sem=t_recv.at[yy],
            device_id=(b, tm_of(u, h, c)), device_id_type=MESH,
        )

    def z_copy(v, hh):
        start = v * 2 * half + hh * half + half - BLOCK
        cols = pl.ds(pl.multiple_of(start, BLOCK), BLOCK)
        return pltpu.make_async_remote_copy(
            src_ref=tsum.at[v, :, 0:BLOCK], dst_ref=out_ref.at[:, cols],
            send_sem=t_send.at[v], recv_sem=z_recv.at[v],
            device_id=(b, tm_of(y, 1 - h, c)), device_id_type=MESH,
        )

    def share_cross(u, carry):
        c_copy(1, u).start()
        return carry

    def share_same(u, carry):
        @pl.when(u >= y)
        def _():
            c_copy(0, u).start()
        return carry

    lax.fori_loop(0, NY, share_cross, 0)
    lax.fori_loop(0, NY, share_same, 0)

    s_copy.wait_recv()
    for u in range(NY + 1):
        total = s_mine[u] + s_oth[u]
        s_tot[u] = total
        s_col[u] = total.T
    count = s_tot[0, 1:2, 0:1] * BLOCK

    def scaled(g, u_row, u_col, cols):
        si = s_col[u_row, mine, 0:1]
        sj = s_tot[u_col, 0:1, cols]
        return g * count / (si * sj)

    def back(u, carry):
        c_copy(1, u).wait_recv()

        @pl.when(jnp.logical_and(u < y, near(u, y)))
        def _():
            tsum[u] = scaled(acc_x[u, mine, :] + rx[u], u, NY, whole)
            t_copy(y, u).start()

        @pl.when(split(u, y))
        def _():
            tsum[u, :, first] = scaled(acc_x[u, mine, first] + rx[u, :, first], u, NY, first)
            t_split(y, u).start()

        @pl.when(split(y, u))
        def _():
            tsum[u, :, 0:BLOCK] = scaled(
                acc_x[u, mine, 0:BLOCK] + rx[u, :, 0:BLOCK], NY, u, last
            )
            z_copy(u, h).start()
        return carry

    lax.fori_loop(0, NY, back, 0)

    tile = lax.broadcasted_iota(jnp.int32, (panel, half), 1)

    def place(u, carry):
        same_cols = pl.ds(pl.multiple_of(u * 2 * half + h * half, half), half)
        cross_cols = pl.ds(pl.multiple_of(u * 2 * half + (1 - h) * half, half), half)

        @pl.when(u < y)
        def _():
            out_ref[:, same_cols] = jnp.zeros((panel, half), jnp.float32)
            out_ref[:, cross_cols] = jnp.zeros((panel, half), jnp.float32)

        @pl.when(u >= y)
        def _():
            c_copy(0, u).wait_recv()
            g = scaled(acc_s[u, mine, :] + rs[u], y, u, whole)
            first_tile = u * 4 + h * 2
            tiles = first_tile + jnp.where(tile >= panel, 1, 0)
            out_ref[:, same_cols] = jnp.where(tiles >= t, g, 0.0)

        @pl.when(u == y)
        def _():
            g = scaled(acc_x[u, mine, :] + rx[u], y, NY, whole)
            first_tile = u * 4 + (1 - h) * 2
            tiles = first_tile + jnp.where(tile >= panel, 1, 0)
            out_ref[:, cross_cols] = jnp.where(tiles >= t, g, 0.0)
        return carry

    lax.fori_loop(0, NY, place, 0)

    def arrive(u, carry):
        @pl.when(jnp.logical_and(u > y, near(y, u)))
        def _():
            t_copy(u, y).wait_recv()

        @pl.when(split(y, u))
        def _():
            t_split(u, y).wait_recv()
            z_copy(u, 1 - h).wait_recv()
        return carry

    lax.fori_loop(0, NY, arrive, 0)

    @pl.when(bp != c)
    def _():
        st_copy(0, 0).wait_send()

    def drain_one(i, carry):
        @pl.when(i >= 1)
        def _():
            st_copy(i, 0).wait_send()
        st_copy(i, 1).wait_send()
        return carry

    lax.fori_loop(0, nblk, drain_one, 0)

    def drain_y(m, carry):
        y_copy(m, 0, y, whole, up).wait_send()
        y_copy(m, 1, y, whole, down).wait_send()
        y_copy(m, 2, down, low, up).wait_send()
        y_copy(m, 3, up, high, down).wait_send()
        return carry

    lax.fori_loop(0, nsrc, drain_y, 0)

    def drain_c(u, carry):
        c_copy(1, u).wait_send()

        @pl.when(u >= y)
        def _():
            c_copy(0, u).wait_send()

        @pl.when(jnp.logical_and(u < y, near(u, y)))
        def _():
            t_copy(y, u).wait_send()

        @pl.when(split(u, y))
        def _():
            t_split(y, u).wait_send()

        @pl.when(split(y, u))
        def _():
            z_copy(u, h).wait_send()
        return carry

    lax.fori_loop(0, NY, drain_c, 0)
    s_copy.wait_send()


def on_device(intensity, block_cycle, cycle_order):
    panel = intensity.shape[0]
    nblk = cycle_order.shape[0]
    nsrc = nblk // 2
    half = 2 * panel
    frames = panel * lax.axis_size("tm")
    vmem = pl.BlockSpec(memory_space=pltpu.VMEM)
    smem = pl.BlockSpec(memory_space=pltpu.SMEM)
    dma = pltpu.SemaphoreType.DMA
    twotime = pl.pallas_call(
        main_kernel,
        out_shape=jax.ShapeDtypeStruct((panel, frames), jnp.float32),
        in_specs=[smem, smem, vmem],
        out_specs=vmem,
        scratch_shapes=[
            pltpu.VMEM((nblk, panel, W), jnp.bfloat16),
            pltpu.VMEM((NY, half, nsrc * W), jnp.bfloat16),
            pltpu.VMEM((half, nsrc * W), jnp.bfloat16),
            pltpu.VMEM((NY, half, half), jnp.float32),
            pltpu.VMEM((NY, half, half), jnp.float32),
            pltpu.VMEM((NY, panel, half), jnp.float32),
            pltpu.VMEM((NY, panel, half), jnp.float32),
            pltpu.VMEM((NY, panel, half), jnp.float32),
            pltpu.VMEM((NY + 1, 8, half), jnp.float32),
            pltpu.VMEM((NY + 1, 8, half), jnp.float32),
            pltpu.VMEM((NY + 1, 8, half), jnp.float32),
            pltpu.VMEM((NY + 1, 8, half), jnp.float32),
            pltpu.VMEM((NY + 1, half, 8), jnp.float32),
            dma((2, nblk)), dma((2, nsrc, 2)),
            dma((nsrc, 4)), dma((nsrc, 4)),
            dma((2, NY)), dma((2, NY)),
            dma((NY,)), dma((NY,)), dma((NY,)),
            dma, dma,
        ],
        compiler_params=pltpu.CompilerParams(
            collective_id=0, has_side_effects=True, vmem_limit_bytes=32 << 20
        ),
        name="exchange",
    )(block_cycle, cycle_order, intensity)
    return twotime.reshape(1, panel, frames)


def solution(mesh):
    placed = (P("tm", "blk"), P("blk"), P())
    return jax.shard_map(
        on_device, mesh=mesh, in_specs=placed, out_specs=P("blk", "tm", None), check_vma=False
    )
```

```python
import jax
import jax.numpy as jnp
from jax import lax
from jax.experimental import pallas as pl
from jax.experimental.pallas import tpu as pltpu
from jax.sharding import PartitionSpec as P

BLOCK = 128
MESH = pl.DeviceIdType.MESH
NY = 4
W = 2 * BLOCK
STRIDE = 7
LAG = 1
AHEAD = 2
CUT = 2


def dot_t(a, b):
    return lax.dot_general(a, b, (((1,), (1,)), ((), ())), preferred_element_type=jnp.float32)


def main_kernel(
    bc_hbm, order_hbm, x_hbm, out_ref,
    bc_ref, order_ref, x_ref, slots, a_buf, o_buf, acc_s, acc_x, rs, rx, tsum, sum_acc, s_mine, s_oth, s_tot, s_col,
    st_send, st_recv, y_send, y_recv, c_send, c_recv, t_send, t_recv, z_recv, s_send, s_recv, in_sem,
):
    nblk, panel, _ = slots.shape
    nsrc = nblk // 2
    b = lax.axis_index("blk")
    t = lax.axis_index("tm")
    c = t % 2
    h = (t // 2) % 2
    y = t // 4
    bp = b % 2
    bm = b // 2
    half = 2 * panel
    up = (y + 1) % NY
    down = (y + NY - 1) % NY
    far = (y + 2) % NY

    def tm_of(yy, hh, cc):
        return (yy * 2 + hh) * 2 + cc

    other = (b, tm_of(y, h, 1 - c))

    inputs = [
        pltpu.make_async_copy(src, dst, in_sem.at[i])
        for i, (src, dst) in enumerate(((bc_hbm, bc_ref), (order_hbm, order_ref), (x_hbm, x_ref)))
    ]
    for copy in inputs:
        copy.start()

    barrier = pltpu.get_barrier_semaphore()

    def greet(k, carry):
        s = (b + k) % nblk
        for j in range(4):
            pl.semaphore_signal(barrier, inc=1, device_id=(s, y * 4 + j), device_id_type=MESH)
        return carry

    lax.fori_loop(1, nblk, greet, 0)
    for j in range(1, 4):
        pl.semaphore_signal(barrier, inc=1, device_id=(b, y * 4 + (t + j) % 4), device_id_type=MESH)
    for r in range(1, NY):
        pl.semaphore_signal(
            barrier, inc=1, device_id=(b, tm_of((y + r) % NY, h, c)), device_id_type=MESH
        )

    blk_dev = x_ref.shape[1] // BLOCK

    def target(i):
        return (b + i * STRIDE) % nblk

    def fill(i, carry):
        s = target(i)
        cyc = order_ref[s]
        first = jnp.int32(-1)
        second = jnp.int32(-1)
        for j in range(blk_dev):
            hit = bc_ref[j] == cyc
            second = jnp.where(jnp.logical_and(hit, first >= 0), j, second)
            first = jnp.where(jnp.logical_and(hit, first < 0), j, first)
        for r, src in ((0, first), (1, second)):
            start = jnp.maximum(src, 0) * BLOCK
            keep = jnp.where(src >= 0, jnp.float32(1.0), jnp.float32(0.0))
            block = x_ref[:, pl.ds(start, BLOCK)].astype(jnp.float32) * keep
            slots[s, :, pl.ds(r * BLOCK, BLOCK)] = block.astype(jnp.bfloat16)
        return carry

    for copy in inputs:
        copy.wait()
    lax.fori_loop(0, AHEAD, fill, 0)

    pl.semaphore_wait(barrier, (nblk - 1) * 4 + 3 + (NY - 1))

    my_rows = pl.ds(pl.multiple_of(c * panel, panel), panel)
    my_cols = pl.ds(pl.multiple_of(bm * W, W), W)

    def st_copy(i, d):
        s = target(i)
        dst = a_buf.at[y, my_rows, my_cols] if d == 0 else o_buf.at[my_rows, my_cols]
        return pltpu.make_async_remote_copy(
            src_ref=slots.at[s],
            dst_ref=dst,
            send_sem=st_send.at[d, i],
            recv_sem=st_recv.at[d, bm, c],
            device_id=(s, tm_of(y, h if d == 0 else 1 - h, bp)),
            device_id_type=MESH,
        )

    @pl.when(bp == c)
    def _():
        pltpu.make_async_copy(
            slots.at[b], a_buf.at[y, my_rows, my_cols], st_recv.at[0, bm, c]
        ).start()

    @pl.when(bp != c)
    def _():
        st_copy(0, 0).start()

    def send_one(i, carry):
        @pl.when(i + AHEAD - 1 < nblk)
        def _():
            fill(i + AHEAD - 1, 0)

        @pl.when(i < nblk)
        def _():
            st_copy(i, 0).start()

        @pl.when(i >= LAG)
        def _():
            st_copy(i - LAG, 1).start()
        return carry

    lax.fori_loop(1, nblk + LAG, send_one, 0)

    def clear(u, carry):
        acc_s[u] = jnp.zeros((half, half), jnp.float32)
        acc_x[u] = jnp.zeros((half, half), jnp.float32)
        return carry

    lax.fori_loop(0, NY, clear, 0)
    sum_acc[...] = jnp.zeros(sum_acc.shape, jnp.float32)

    def st_wait(d, m, q):
        rows = pl.ds(q * panel, panel)
        cols = pl.ds(pl.multiple_of(m * W, W), W)
        dst = a_buf.at[y, rows, cols] if d == 0 else o_buf.at[rows, cols]
        pltpu.make_async_remote_copy(
            src_ref=slots.at[0], dst_ref=dst, send_sem=st_send.at[d, 0], recv_sem=st_recv.at[d, m, q],
            device_id=other, device_id_type=MESH,
        ).wait_recv()

    whole = pl.ds(0, half)

    def y_copy(m, way, src_y, q, to_y):
        rows = pl.ds(q * panel, panel)
        cols = pl.ds(pl.multiple_of(m * W, W), W)
        return pltpu.make_async_remote_copy(
            src_ref=a_buf.at[src_y, rows, cols],
            dst_ref=a_buf.at[src_y, rows, cols],
            send_sem=y_send.at[m, way],
            recv_sem=y_recv.at[m, way],
            device_id=(b, tm_of(to_y, h, c)),
            device_id_type=MESH,
        )

    def source(j):
        k = (2 * j + (b + c) % 2) * STRIDE % nblk
        return ((b + nblk - k) % nblk) // 2

    ones = jnp.ones((8, W), jnp.bfloat16)

    first = pl.ds(0, half - BLOCK)
    last = pl.ds(half - BLOCK, BLOCK)

    def split(u, v):
        return jnp.logical_and(u < CUT, v >= CUT)

    def near(u, v):
        return jnp.logical_and(u <= v, jnp.logical_or(u >= CUT, v < CUT))

    def job(m, u):
        cols = pl.ds(pl.multiple_of(m * W, W), W)
        panel_u = a_buf[u, :, cols]
        sum_acc[u] += dot_t(ones, panel_u)

        @pl.when(near(u, y))
        def _():
            acc_x[u] += dot_t(panel_u, o_buf[:, cols])

        @pl.when(split(u, y))
        def _():
            acc_x[u, :, first] += dot_t(panel_u, o_buf[first, cols])

        @pl.when(split(y, u))
        def _():
            acc_x[u, :, 0:BLOCK] += dot_t(o_buf[:, cols], a_buf[u, last, cols])

        @pl.when(u >= y)
        def _():
            acc_s[u] += dot_t(a_buf[y, :, cols], panel_u)

    def neighbour(r):
        return (y + r + r // 2) % NY

    def multiply_near(m):
        cols = pl.ds(pl.multiple_of(m * W, W), W)
        sum_acc[NY] += dot_t(ones, o_buf[:, cols])

        def one(r, carry):
            job(m, neighbour(r))
            return carry

        lax.fori_loop(0, 3, one, 0)

    def multiply_far(m):
        y_copy(m, 4, far, 0, y).wait_recv()
        y_copy(m, 5, far, 1, y).wait_recv()
        job(m, far)

    def step(j, carry):
        @pl.when(j < nsrc)
        def _():
            m = source(j)
            st_wait(0, m, 0)
            y_copy(m, 0, y, 0, up).start()
            st_wait(0, m, 1)
            y_copy(m, 3, y, 1, down).start()
            y_copy(m, 1, y, 1, up).start()
            y_copy(m, 2, y, 0, down).start()

        @pl.when(j >= 1)
        def _():
            m = source(j - 1)
            y_copy(m, 0, down, 0, y).wait_recv()
            y_copy(m, 4, down, 0, up).start()
            y_copy(m, 3, up, 1, y).wait_recv()
            y_copy(m, 5, up, 1, down).start()

        @pl.when(j >= 2)
        def _():
            multiply_far(source(j - 2))

        @pl.when(j >= 1)
        def _():
            m = source(j - 1)
            y_copy(m, 1, down, 1, y).wait_recv()
            y_copy(m, 2, up, 0, y).wait_recv()
            for q in range(2):
                st_wait(1, m, q)
            multiply_near(m)
        return carry

    lax.fori_loop(0, nsrc + 1, step, 0)

    theirs = pl.ds(pl.multiple_of((1 - c) * panel, panel), panel)
    mine = pl.ds(pl.multiple_of(c * panel, panel), panel)

    head = a_buf[y, 0:16, :].astype(jnp.float32)
    lane = lax.broadcasted_iota(jnp.int32, head.shape, 1)
    row = lax.broadcasted_iota(jnp.int32, head.shape, 0)
    mark = jnp.where(jnp.logical_and(lane % BLOCK == 0, row == 0), head, 0.0)
    filled = jnp.sum(jnp.where(mark > 0.0, 1.0, 0.0))
    srow = lax.broadcasted_iota(jnp.int32, (8, half), 0)

    def s_copy(u):
        return pltpu.make_async_remote_copy(
            src_ref=s_mine.at[u], dst_ref=s_oth.at[u], send_sem=s_send.at[u], recv_sem=s_recv.at[u],
            device_id=other, device_id_type=MESH,
        )

    def share_sum(u):
        s_mine[u] = jnp.where(srow == 1, filled, sum_acc[u])
        s_copy(u).start()

    def take_sum(u):
        s_copy(u).wait_recv()
        total = s_mine[u] + s_oth[u]
        s_tot[u] = total
        s_col[u] = total.T

    def c_copy(kind, u):
        src, dst = (acc_s, rs) if kind == 0 else (acc_x, rx)
        return pltpu.make_async_remote_copy(
            src_ref=src.at[u, theirs, :], dst_ref=dst.at[u],
            send_sem=c_send.at[kind, u], recv_sem=c_recv.at[kind, u],
            device_id=other, device_id_type=MESH,
        )

    def t_copy(yy, u):
        cols = pl.ds(pl.multiple_of(yy * 2 * half + (1 - h) * half, half), half)
        return pltpu.make_async_remote_copy(
            src_ref=tsum.at[u], dst_ref=out_ref.at[:, cols],
            send_sem=t_send.at[u], recv_sem=t_recv.at[yy],
            device_id=(b, tm_of(u, h, c)), device_id_type=MESH,
        )

    def t_split(yy, u):
        start = yy * 2 * half + (1 - h) * half
        cols = pl.ds(pl.multiple_of(start, BLOCK), half - BLOCK)
        return pltpu.make_async_remote_copy(
            src_ref=tsum.at[u, :, first], dst_ref=out_ref.at[:, cols],
            send_sem=t_send.at[u], recv_sem=t_recv.at[yy],
            device_id=(b, tm_of(u, h, c)), device_id_type=MESH,
        )

    def z_copy(v, hh):
        start = v * 2 * half + hh * half + half - BLOCK
        cols = pl.ds(pl.multiple_of(start, BLOCK), BLOCK)
        return pltpu.make_async_remote_copy(
            src_ref=tsum.at[v, :, 0:BLOCK], dst_ref=out_ref.at[:, cols],
            send_sem=t_send.at[v], recv_sem=z_recv.at[v],
            device_id=(b, tm_of(y, 1 - h, c)), device_id_type=MESH,
        )

    def share(u):
        c_copy(1, u).start()

        @pl.when(u >= y)
        def _():
            c_copy(0, u).start()

    def scaled(g, u_row, u_col, cols):
        si = s_col[u_row, mine, 0:1]
        sj = s_tot[u_col, 0:1, cols]
        return g * (s_tot[NY, 1:2, 0:1] * BLOCK) / (si * sj)

    def back(u):
        c_copy(1, u).wait_recv()

        @pl.when(jnp.logical_and(u < y, near(u, y)))
        def _():
            tsum[u] = scaled(acc_x[u, mine, :] + rx[u], u, NY, whole)
            t_copy(y, u).start()

        @pl.when(split(u, y))
        def _():
            tsum[u, :, first] = scaled(acc_x[u, mine, first] + rx[u, :, first], u, NY, first)
            t_split(y, u).start()

        @pl.when(split(y, u))
        def _():
            tsum[u, :, 0:BLOCK] = scaled(
                acc_x[u, mine, 0:BLOCK] + rx[u, :, 0:BLOCK], NY, u, last
            )
            z_copy(u, h).start()

    share_sum(NY)

    def share_near(r, carry):
        share_sum(neighbour(r))
        return carry

    def share_blocks(r, carry):
        share(neighbour(r))
        return carry

    def take_near(r, carry):
        take_sum(neighbour(r))
        return carry

    def back_near(r, carry):
        back(neighbour(r))
        return carry

    lax.fori_loop(0, 3, share_near, 0)
    lax.fori_loop(0, 3, share_blocks, 0)
    take_sum(NY)
    lax.fori_loop(0, 3, take_near, 0)
    lax.fori_loop(0, 3, back_near, 0)
    multiply_far(source(nsrc - 1))
    share_sum(far)
    share(far)
    take_sum(far)
    back(far)

    tile = lax.broadcasted_iota(jnp.int32, (panel, half), 1)

    def place(u, carry):
        same_cols = pl.ds(pl.multiple_of(u * 2 * half + h * half, half), half)
        cross_cols = pl.ds(pl.multiple_of(u * 2 * half + (1 - h) * half, half), half)

        @pl.when(u < y)
        def _():
            out_ref[:, same_cols] = jnp.zeros((panel, half), jnp.float32)
            out_ref[:, cross_cols] = jnp.zeros((panel, half), jnp.float32)

        @pl.when(u >= y)
        def _():
            c_copy(0, u).wait_recv()
            g = scaled(acc_s[u, mine, :] + rs[u], y, u, whole)
            first_tile = u * 4 + h * 2
            tiles = first_tile + jnp.where(tile >= panel, 1, 0)
            out_ref[:, same_cols] = jnp.where(tiles >= t, g, 0.0)

        @pl.when(u == y)
        def _():
            g = scaled(acc_x[u, mine, :] + rx[u], y, NY, whole)
            first_tile = u * 4 + (1 - h) * 2
            tiles = first_tile + jnp.where(tile >= panel, 1, 0)
            out_ref[:, cross_cols] = jnp.where(tiles >= t, g, 0.0)
        return carry

    lax.fori_loop(0, NY, place, 0)

    def arrive(u, carry):
        @pl.when(jnp.logical_and(u > y, near(y, u)))
        def _():
            t_copy(u, y).wait_recv()

        @pl.when(split(y, u))
        def _():
            t_split(u, y).wait_recv()
            z_copy(u, 1 - h).wait_recv()
        return carry

    lax.fori_loop(0, NY, arrive, 0)

    @pl.when(bp != c)
    def _():
        st_copy(0, 0).wait_send()

    def drain_one(i, carry):
        @pl.when(i >= 1)
        def _():
            st_copy(i, 0).wait_send()
        st_copy(i, 1).wait_send()
        return carry

    lax.fori_loop(0, nblk, drain_one, 0)

    def drain_y(m, carry):
        y_copy(m, 0, y, 0, up).wait_send()
        y_copy(m, 1, y, 1, up).wait_send()
        y_copy(m, 2, y, 0, down).wait_send()
        y_copy(m, 3, y, 1, down).wait_send()
        y_copy(m, 4, down, 0, up).wait_send()
        y_copy(m, 5, up, 1, down).wait_send()
        return carry

    lax.fori_loop(0, nsrc, drain_y, 0)

    def drain_c(u, carry):
        c_copy(1, u).wait_send()

        @pl.when(u >= y)
        def _():
            c_copy(0, u).wait_send()

        @pl.when(jnp.logical_and(u < y, near(u, y)))
        def _():
            t_copy(y, u).wait_send()

        @pl.when(split(u, y))
        def _():
            t_split(y, u).wait_send()

        @pl.when(split(y, u))
        def _():
            z_copy(u, h).wait_send()
        return carry

    lax.fori_loop(0, NY, drain_c, 0)
    for u in range(NY + 1):
        s_copy(u).wait_send()


def on_device(intensity, block_cycle, cycle_order):
    panel = intensity.shape[0]
    nblk = cycle_order.shape[0]
    nsrc = nblk // 2
    half = 2 * panel
    frames = panel * lax.axis_size("tm")
    vmem = pl.BlockSpec(memory_space=pltpu.VMEM)
    hbm = pl.BlockSpec(memory_space=pltpu.HBM)
    dma = pltpu.SemaphoreType.DMA
    twotime = pl.pallas_call(
        main_kernel,
        out_shape=jax.ShapeDtypeStruct((panel, frames), jnp.float32),
        in_specs=[hbm, hbm, hbm],
        out_specs=vmem,
        scratch_shapes=[
            pltpu.SMEM(block_cycle.shape, jnp.int32),
            pltpu.SMEM(cycle_order.shape, jnp.int32),
            pltpu.VMEM(intensity.shape, jnp.bfloat16),
            pltpu.VMEM((nblk, panel, W), jnp.bfloat16),
            pltpu.VMEM((NY, half, nsrc * W), jnp.bfloat16),
            pltpu.VMEM((half, nsrc * W), jnp.bfloat16),
            pltpu.VMEM((NY, half, half), jnp.float32),
            pltpu.VMEM((NY, half, half), jnp.float32),
            pltpu.VMEM((NY, panel, half), jnp.float32),
            pltpu.VMEM((NY, panel, half), jnp.float32),
            pltpu.VMEM((NY, panel, half), jnp.float32),
            pltpu.VMEM((NY + 1, 8, half), jnp.float32),
            pltpu.VMEM((NY + 1, 8, half), jnp.float32),
            pltpu.VMEM((NY + 1, 8, half), jnp.float32),
            pltpu.VMEM((NY + 1, 8, half), jnp.float32),
            pltpu.VMEM((NY + 1, half, 8), jnp.float32),
            dma((2, nblk)), dma((2, nsrc, 2)),
            dma((nsrc, 6)), dma((nsrc, 6)),
            dma((2, NY)), dma((2, NY)),
            dma((NY,)), dma((NY,)), dma((NY,)),
            dma((NY + 1,)), dma((NY + 1,)), dma((3,)),
        ],
        compiler_params=pltpu.CompilerParams(
            collective_id=0, has_side_effects=True, vmem_limit_bytes=32 << 20
        ),
        name="exchange",
    )(*(pltpu.with_memory_space_constraint(a, pltpu.HBM) for a in (block_cycle, cycle_order, intensity)))
    return twotime.reshape(1, panel, frames)


def solution(mesh):
    placed = (P("tm", "blk"), P("blk"), P())
    return jax.shard_map(
        on_device, mesh=mesh, in_specs=placed, out_specs=P("blk", "tm", None), check_vma=False
    )
```

```python
import jax
import jax.numpy as jnp
from jax import lax
from jax.experimental import pallas as pl
from jax.experimental.pallas import tpu as pltpu
from jax.sharding import PartitionSpec as P

BLOCK = 128
MESH = pl.DeviceIdType.MESH
NY = 4
W = 2 * BLOCK
STRIDE = 7
LAG = 1
AHEAD = 2
CUT = 2


def dot_t(a, b):
    return lax.dot_general(a, b, (((1,), (1,)), ((), ())), preferred_element_type=jnp.float32)


def main_kernel(
    bc_hbm, order_hbm, x_hbm, out_ref,
    bc_ref, order_ref, x_ref, slots, a_buf, o_buf, acc_s, acc_x, rs, rx, tsum, sum_acc, s_mine, s_oth, s_tot, s_col,
    st_send, st_recv, y_send, y_recv, c_send, c_recv, t_send, t_recv, z_recv, s_send, s_recv, in_sem,
):
    nblk, panel, _ = slots.shape
    nsrc = nblk // 2
    b = lax.axis_index("blk")
    t = lax.axis_index("tm")
    c = t % 2
    h = (t // 2) % 2
    y = t // 4
    bp = b % 2
    bm = b // 2
    half = 2 * panel
    up = (y + 1) % NY
    down = (y + NY - 1) % NY
    far = (y + 2) % NY

    def tm_of(yy, hh, cc):
        return (yy * 2 + hh) * 2 + cc

    other = (b, tm_of(y, h, 1 - c))

    inputs = [
        pltpu.make_async_copy(src, dst, in_sem.at[i])
        for i, (src, dst) in enumerate(((bc_hbm, bc_ref), (order_hbm, order_ref), (x_hbm, x_ref)))
    ]
    for copy in inputs:
        copy.start()

    barrier = pltpu.get_barrier_semaphore()

    def greet(k, carry):
        s = (b + k) % nblk
        for j in range(4):
            pl.semaphore_signal(barrier, inc=1, device_id=(s, y * 4 + j), device_id_type=MESH)
        return carry

    lax.fori_loop(1, nblk, greet, 0)
    for j in range(1, 4):
        pl.semaphore_signal(barrier, inc=1, device_id=(b, y * 4 + (t + j) % 4), device_id_type=MESH)
    for r in range(1, NY):
        pl.semaphore_signal(
            barrier, inc=1, device_id=(b, tm_of((y + r) % NY, h, c)), device_id_type=MESH
        )

    blk_dev = x_ref.shape[1] // BLOCK

    def target(i):
        return (b + i * STRIDE) % nblk

    def fill(i, carry):
        s = target(i)
        cyc = order_ref[s]
        first = jnp.int32(-1)
        second = jnp.int32(-1)
        for j in range(blk_dev):
            hit = bc_ref[j] == cyc
            second = jnp.where(jnp.logical_and(hit, first >= 0), j, second)
            first = jnp.where(jnp.logical_and(hit, first < 0), j, first)
        for r, src in ((0, first), (1, second)):
            start = jnp.maximum(src, 0) * BLOCK
            keep = jnp.where(src >= 0, jnp.float32(1.0), jnp.float32(0.0))
            block = x_ref[:, pl.ds(start, BLOCK)].astype(jnp.float32) * keep
            slots[s, :, pl.ds(r * BLOCK, BLOCK)] = block.astype(jnp.bfloat16)
        return carry

    for copy in inputs:
        copy.wait()
    lax.fori_loop(0, AHEAD, fill, 0)

    pl.semaphore_wait(barrier, (nblk - 1) * 4 + 3 + (NY - 1))

    my_rows = pl.ds(pl.multiple_of(c * panel, panel), panel)
    my_cols = pl.ds(pl.multiple_of(bm * W, W), W)

    def st_copy(i, d):
        s = target(i)
        dst = a_buf.at[y, my_rows, my_cols] if d == 0 else o_buf.at[my_rows, my_cols]
        return pltpu.make_async_remote_copy(
            src_ref=slots.at[s],
            dst_ref=dst,
            send_sem=st_send.at[d, i],
            recv_sem=st_recv.at[d, bm, c],
            device_id=(s, tm_of(y, h if d == 0 else 1 - h, bp)),
            device_id_type=MESH,
        )

    @pl.when(bp == c)
    def _():
        pltpu.make_async_copy(
            slots.at[b], a_buf.at[y, my_rows, my_cols], st_recv.at[0, bm, c]
        ).start()

    @pl.when(bp != c)
    def _():
        st_copy(0, 0).start()

    def send_one(i, carry):
        @pl.when(i + AHEAD - 1 < nblk)
        def _():
            fill(i + AHEAD - 1, 0)

        @pl.when(i < nblk)
        def _():
            st_copy(i, 0).start()

        @pl.when(i >= LAG)
        def _():
            st_copy(i - LAG, 1).start()
        return carry

    lax.fori_loop(1, nblk + LAG, send_one, 0)

    def clear(u, carry):
        acc_s[u] = jnp.zeros((half, half), jnp.float32)
        acc_x[u] = jnp.zeros((half, half), jnp.float32)
        return carry

    lax.fori_loop(0, NY, clear, 0)
    sum_acc[...] = jnp.zeros(sum_acc.shape, jnp.float32)

    def st_wait(d, m, q):
        rows = pl.ds(q * panel, panel)
        cols = pl.ds(pl.multiple_of(m * W, W), W)
        dst = a_buf.at[y, rows, cols] if d == 0 else o_buf.at[rows, cols]
        pltpu.make_async_remote_copy(
            src_ref=slots.at[0], dst_ref=dst, send_sem=st_send.at[d, 0], recv_sem=st_recv.at[d, m, q],
            device_id=other, device_id_type=MESH,
        ).wait_recv()

    whole = pl.ds(0, half)

    def y_copy(m, way, src_y, q, to_y):
        rows = pl.ds(q * panel, panel)
        cols = pl.ds(pl.multiple_of(m * W, W), W)
        return pltpu.make_async_remote_copy(
            src_ref=a_buf.at[src_y, rows, cols],
            dst_ref=a_buf.at[src_y, rows, cols],
            send_sem=y_send.at[m, way],
            recv_sem=y_recv.at[m, way],
            device_id=(b, tm_of(to_y, h, c)),
            device_id_type=MESH,
        )

    def source(j):
        k = (2 * j + (b + c) % 2) * STRIDE % nblk
        return ((b + nblk - k) % nblk) // 2

    ones = jnp.ones((8, W), jnp.bfloat16)

    first = pl.ds(0, half - BLOCK)
    last = pl.ds(half - BLOCK, BLOCK)

    def split(u, v):
        return jnp.logical_and(u < CUT, v >= CUT)

    def near(u, v):
        return jnp.logical_and(u <= v, jnp.logical_or(u >= CUT, v < CUT))

    def job_sum(m, u):
        cols = pl.ds(pl.multiple_of(m * W, W), W)
        sum_acc[u] += dot_t(ones, a_buf[u, :, cols])

    def job_cross(m, u):
        cols = pl.ds(pl.multiple_of(m * W, W), W)

        @pl.when(near(u, y))
        def _():
            acc_x[u] += dot_t(a_buf[u, :, cols], o_buf[:, cols])

        @pl.when(split(u, y))
        def _():
            acc_x[u, :, first] += dot_t(a_buf[u, :, cols], o_buf[first, cols])

        @pl.when(split(y, u))
        def _():
            acc_x[u, :, 0:BLOCK] += dot_t(o_buf[:, cols], a_buf[u, last, cols])

    def job_same(m, u):
        cols = pl.ds(pl.multiple_of(m * W, W), W)

        @pl.when(u >= y)
        def _():
            acc_s[u] += dot_t(a_buf[y, :, cols], a_buf[u, :, cols])

    def job(m, u):
        job_sum(m, u)
        job_cross(m, u)
        job_same(m, u)

    def neighbour(r):
        return (y + r + r // 2) % NY

    def other_sum(m):
        cols = pl.ds(pl.multiple_of(m * W, W), W)
        sum_acc[NY] += dot_t(ones, o_buf[:, cols])

    def await_near(m):
        y_copy(m, 1, down, 1, y).wait_recv()
        y_copy(m, 2, up, 0, y).wait_recv()
        for q in range(2):
            st_wait(1, m, q)

    def multiply_near(m):
        other_sum(m)

        def one(r, carry):
            job(m, neighbour(r))
            return carry

        lax.fori_loop(0, 3, one, 0)

    def multiply_far(m):
        y_copy(m, 4, far, 0, y).wait_recv()
        y_copy(m, 5, far, 1, y).wait_recv()
        job(m, far)

    def step(j, carry):
        @pl.when(j < nsrc)
        def _():
            m = source(j)
            st_wait(0, m, 0)
            y_copy(m, 0, y, 0, up).start()
            st_wait(0, m, 1)
            y_copy(m, 3, y, 1, down).start()
            y_copy(m, 1, y, 1, up).start()
            y_copy(m, 2, y, 0, down).start()

        @pl.when(j >= 1)
        def _():
            m = source(j - 1)
            y_copy(m, 0, down, 0, y).wait_recv()
            y_copy(m, 4, down, 0, up).start()
            y_copy(m, 3, up, 1, y).wait_recv()
            y_copy(m, 5, up, 1, down).start()

        @pl.when(j >= 2)
        def _():
            multiply_far(source(j - 2))

        @pl.when(jnp.logical_and(j >= 1, j < nsrc))
        def _():
            m = source(j - 1)
            await_near(m)
            multiply_near(m)
        return carry

    lax.fori_loop(0, nsrc + 1, step, 0)

    theirs = pl.ds(pl.multiple_of((1 - c) * panel, panel), panel)
    mine = pl.ds(pl.multiple_of(c * panel, panel), panel)

    end = source(nsrc - 1)
    head = a_buf[y, 0:16, :].astype(jnp.float32)
    lane = lax.broadcasted_iota(jnp.int32, head.shape, 1)
    row = lax.broadcasted_iota(jnp.int32, head.shape, 0)
    mark = jnp.where(jnp.logical_and(lane % BLOCK == 0, row == 0), head, 0.0)
    filled = jnp.sum(jnp.where(mark > 0.0, 1.0, 0.0))
    srow = lax.broadcasted_iota(jnp.int32, (8, half), 0)

    def s_copy(u):
        return pltpu.make_async_remote_copy(
            src_ref=s_mine.at[u], dst_ref=s_oth.at[u], send_sem=s_send.at[u], recv_sem=s_recv.at[u],
            device_id=other, device_id_type=MESH,
        )

    def share_sum(u):
        s_mine[u] = jnp.where(srow == 1, filled, sum_acc[u])
        s_copy(u).start()

    def take_sum(u):
        s_copy(u).wait_recv()
        total = s_mine[u] + s_oth[u]
        s_tot[u] = total
        s_col[u] = total.T

    def c_copy(kind, u):
        src, dst = (acc_s, rs) if kind == 0 else (acc_x, rx)
        return pltpu.make_async_remote_copy(
            src_ref=src.at[u, theirs, :], dst_ref=dst.at[u],
            send_sem=c_send.at[kind, u], recv_sem=c_recv.at[kind, u],
            device_id=other, device_id_type=MESH,
        )

    def t_copy(yy, u):
        cols = pl.ds(pl.multiple_of(yy * 2 * half + (1 - h) * half, half), half)
        return pltpu.make_async_remote_copy(
            src_ref=tsum.at[u], dst_ref=out_ref.at[:, cols],
            send_sem=t_send.at[u], recv_sem=t_recv.at[yy],
            device_id=(b, tm_of(u, h, c)), device_id_type=MESH,
        )

    def t_split(yy, u):
        start = yy * 2 * half + (1 - h) * half
        cols = pl.ds(pl.multiple_of(start, BLOCK), half - BLOCK)
        return pltpu.make_async_remote_copy(
            src_ref=tsum.at[u, :, first], dst_ref=out_ref.at[:, cols],
            send_sem=t_send.at[u], recv_sem=t_recv.at[yy],
            device_id=(b, tm_of(u, h, c)), device_id_type=MESH,
        )

    def z_copy(v, hh):
        start = v * 2 * half + hh * half + half - BLOCK
        cols = pl.ds(pl.multiple_of(start, BLOCK), BLOCK)
        return pltpu.make_async_remote_copy(
            src_ref=tsum.at[v, :, 0:BLOCK], dst_ref=out_ref.at[:, cols],
            send_sem=t_send.at[v], recv_sem=z_recv.at[v],
            device_id=(b, tm_of(y, 1 - h, c)), device_id_type=MESH,
        )

    def share_same(u):
        @pl.when(u >= y)
        def _():
            c_copy(0, u).start()

    def scaled(g, u_row, u_col, cols):
        si = s_col[u_row, mine, 0:1]
        sj = s_tot[u_col, 0:1, cols]
        return g * (s_tot[NY, 1:2, 0:1] * BLOCK) / (si * sj)

    def back(u):
        c_copy(1, u).wait_recv()

        @pl.when(jnp.logical_and(u < y, near(u, y)))
        def _():
            tsum[u] = scaled(acc_x[u, mine, :] + rx[u], u, NY, whole)
            t_copy(y, u).start()

        @pl.when(split(u, y))
        def _():
            tsum[u, :, first] = scaled(acc_x[u, mine, first] + rx[u, :, first], u, NY, first)
            t_split(y, u).start()

        @pl.when(split(y, u))
        def _():
            tsum[u, :, 0:BLOCK] = scaled(
                acc_x[u, mine, 0:BLOCK] + rx[u, :, 0:BLOCK], NY, u, last
            )
            z_copy(u, h).start()

    await_near(end)
    other_sum(end)
    share_sum(NY)

    def near_sum(r, carry):
        job_sum(end, neighbour(r))
        share_sum(neighbour(r))
        return carry

    def near_cross(r, carry):
        job_cross(end, neighbour(r))
        c_copy(1, neighbour(r)).start()
        return carry

    def near_same(r, carry):
        job_same(end, neighbour(r))
        share_same(neighbour(r))
        return carry

    def near_take(r, carry):
        take_sum(neighbour(r))
        return carry

    def near_back(r, carry):
        back(neighbour(r))
        return carry

    lax.fori_loop(0, 3, near_sum, 0)
    lax.fori_loop(0, 3, near_cross, 0)
    lax.fori_loop(0, 3, near_same, 0)
    take_sum(NY)
    lax.fori_loop(0, 3, near_take, 0)
    lax.fori_loop(0, 3, near_back, 0)
    y_copy(end, 4, far, 0, y).wait_recv()
    y_copy(end, 5, far, 1, y).wait_recv()
    job_sum(end, far)
    share_sum(far)
    job_cross(end, far)
    c_copy(1, far).start()
    job_same(end, far)
    share_same(far)
    take_sum(far)
    back(far)

    tile = lax.broadcasted_iota(jnp.int32, (panel, half), 1)

    def place(u, carry):
        same_cols = pl.ds(pl.multiple_of(u * 2 * half + h * half, half), half)
        cross_cols = pl.ds(pl.multiple_of(u * 2 * half + (1 - h) * half, half), half)

        @pl.when(u < y)
        def _():
            out_ref[:, same_cols] = jnp.zeros((panel, half), jnp.float32)
            out_ref[:, cross_cols] = jnp.zeros((panel, half), jnp.float32)

        @pl.when(u >= y)
        def _():
            c_copy(0, u).wait_recv()
            g = scaled(acc_s[u, mine, :] + rs[u], y, u, whole)
            first_tile = u * 4 + h * 2
            tiles = first_tile + jnp.where(tile >= panel, 1, 0)
            out_ref[:, same_cols] = jnp.where(tiles >= t, g, 0.0)

        @pl.when(u == y)
        def _():
            g = scaled(acc_x[u, mine, :] + rx[u], y, NY, whole)
            first_tile = u * 4 + (1 - h) * 2
            tiles = first_tile + jnp.where(tile >= panel, 1, 0)
            out_ref[:, cross_cols] = jnp.where(tiles >= t, g, 0.0)
        return carry

    lax.fori_loop(0, NY, place, 0)

    @pl.when(bp != c)
    def _():
        st_copy(0, 0).wait_send()

    def drain_one(i, carry):
        @pl.when(i >= 1)
        def _():
            st_copy(i, 0).wait_send()
        st_copy(i, 1).wait_send()
        return carry

    lax.fori_loop(0, nblk, drain_one, 0)

    def drain_y(m, carry):
        y_copy(m, 0, y, 0, up).wait_send()
        y_copy(m, 1, y, 1, up).wait_send()
        y_copy(m, 2, y, 0, down).wait_send()
        y_copy(m, 3, y, 1, down).wait_send()
        y_copy(m, 4, down, 0, up).wait_send()
        y_copy(m, 5, up, 1, down).wait_send()
        return carry

    lax.fori_loop(0, nsrc, drain_y, 0)

    def arrive(u, carry):
        @pl.when(jnp.logical_and(u > y, near(y, u)))
        def _():
            t_copy(u, y).wait_recv()

        @pl.when(split(y, u))
        def _():
            t_split(u, y).wait_recv()
            z_copy(u, 1 - h).wait_recv()
        return carry

    lax.fori_loop(0, NY, arrive, 0)

    def drain_c(u, carry):
        c_copy(1, u).wait_send()

        @pl.when(u >= y)
        def _():
            c_copy(0, u).wait_send()

        @pl.when(jnp.logical_and(u < y, near(u, y)))
        def _():
            t_copy(y, u).wait_send()

        @pl.when(split(u, y))
        def _():
            t_split(y, u).wait_send()

        @pl.when(split(y, u))
        def _():
            z_copy(u, h).wait_send()
        return carry

    lax.fori_loop(0, NY, drain_c, 0)
    for u in range(NY + 1):
        s_copy(u).wait_send()


def on_device(intensity, block_cycle, cycle_order):
    panel = intensity.shape[0]
    nblk = cycle_order.shape[0]
    nsrc = nblk // 2
    half = 2 * panel
    frames = panel * lax.axis_size("tm")
    vmem = pl.BlockSpec(memory_space=pltpu.VMEM)
    hbm = pl.BlockSpec(memory_space=pltpu.HBM)
    dma = pltpu.SemaphoreType.DMA
    twotime = pl.pallas_call(
        main_kernel,
        out_shape=jax.ShapeDtypeStruct((panel, frames), jnp.float32),
        in_specs=[hbm, hbm, hbm],
        out_specs=vmem,
        scratch_shapes=[
            pltpu.SMEM(block_cycle.shape, jnp.int32),
            pltpu.SMEM(cycle_order.shape, jnp.int32),
            pltpu.VMEM(intensity.shape, jnp.bfloat16),
            pltpu.VMEM((nblk, panel, W), jnp.bfloat16),
            pltpu.VMEM((NY, half, nsrc * W), jnp.bfloat16),
            pltpu.VMEM((half, nsrc * W), jnp.bfloat16),
            pltpu.VMEM((NY, half, half), jnp.float32),
            pltpu.VMEM((NY, half, half), jnp.float32),
            pltpu.VMEM((NY, panel, half), jnp.float32),
            pltpu.VMEM((NY, panel, half), jnp.float32),
            pltpu.VMEM((NY, panel, half), jnp.float32),
            pltpu.VMEM((NY + 1, 8, half), jnp.float32),
            pltpu.VMEM((NY + 1, 8, half), jnp.float32),
            pltpu.VMEM((NY + 1, 8, half), jnp.float32),
            pltpu.VMEM((NY + 1, 8, half), jnp.float32),
            pltpu.VMEM((NY + 1, half, 8), jnp.float32),
            dma((2, nblk)), dma((2, nsrc, 2)),
            dma((nsrc, 6)), dma((nsrc, 6)),
            dma((2, NY)), dma((2, NY)),
            dma((NY,)), dma((NY,)), dma((NY,)),
            dma((NY + 1,)), dma((NY + 1,)), dma((3,)),
        ],
        compiler_params=pltpu.CompilerParams(
            collective_id=0, has_side_effects=True, vmem_limit_bytes=32 << 20
        ),
        name="exchange",
    )(*(pltpu.with_memory_space_constraint(a, pltpu.HBM) for a in (block_cycle, cycle_order, intensity)))
    return twotime.reshape(1, panel, frames)


def solution(mesh):
    placed = (P("tm", "blk"), P("blk"), P())
    return jax.shard_map(
        on_device, mesh=mesh, in_specs=placed, out_specs=P("blk", "tm", None), check_vma=False
    )
```

```python
import jax
import jax.numpy as jnp
from jax import lax
from jax.experimental import pallas as pl
from jax.experimental.pallas import tpu as pltpu
from jax.sharding import PartitionSpec as P

BLOCK = 128
MESH = pl.DeviceIdType.MESH
NY = 4
W = 2 * BLOCK
STRIDE = 7
LAG = 1
AHEAD = 2
CUT = 2


def dot_t(a, b):
    return lax.dot_general(a, b, (((1,), (1,)), ((), ())), preferred_element_type=jnp.float32)


def main_kernel(
    bc_hbm, order_hbm, x_hbm, out_ref,
    bc_ref, order_ref, x_ref, slots, a_buf, o_buf, acc_s, acc_x, rs, rx, tsum, sum_acc, s_mine, s_oth, s_tot, s_col,
    st_send, st_recv, y_send, y_recv, c_send, c_recv, t_send, t_recv, z_recv, s_send, s_recv, in_sem,
):
    nblk, panel, _ = slots.shape
    nsrc = nblk // 2
    b = lax.axis_index("blk")
    t = lax.axis_index("tm")
    c = t % 2
    h = (t // 2) % 2
    y = t // 4
    bp = b % 2
    bm = b // 2
    half = 2 * panel
    up = (y + 1) % NY
    down = (y + NY - 1) % NY
    far = (y + 2) % NY

    def tm_of(yy, hh, cc):
        return (yy * 2 + hh) * 2 + cc

    other = (b, tm_of(y, h, 1 - c))

    inputs = [
        pltpu.make_async_copy(src, dst, in_sem.at[i])
        for i, (src, dst) in enumerate(((bc_hbm, bc_ref), (order_hbm, order_ref), (x_hbm, x_ref)))
    ]
    for copy in inputs:
        copy.start()

    barrier = pltpu.get_barrier_semaphore()

    def greet(k, carry):
        s = (bm + k) % nsrc * 2 + c
        for j in range(4):
            pl.semaphore_signal(barrier, inc=1, device_id=(s, y * 4 + j), device_id_type=MESH)
        return carry

    @pl.when(bp == c)
    def _():
        for j in range(1, 4):
            to = (b, y * 4 + (t + j) % 4)
            pl.semaphore_signal(barrier, inc=1, device_id=to, device_id_type=MESH)

    @pl.when(bp != c)
    def _():
        greet(0, 0)
        pl.semaphore_signal(barrier, inc=1, device_id=other, device_id_type=MESH)
        to = (b, tm_of(y, 1 - h, c))
        pl.semaphore_signal(barrier, inc=1, device_id=to, device_id_type=MESH)

    lax.fori_loop(1, nsrc, greet, 0)
    for r in range(1, NY):
        pl.semaphore_signal(
            barrier, inc=1, device_id=(b, tm_of((y + r) % NY, h, c)), device_id_type=MESH
        )

    blk_dev = x_ref.shape[1] // BLOCK

    def target(i):
        return (b + i * STRIDE) % nblk

    def fill(i, carry):
        s = target(i)
        cyc = order_ref[s]
        first = jnp.int32(-1)
        second = jnp.int32(-1)
        for j in range(blk_dev):
            hit = bc_ref[j] == cyc
            second = jnp.where(jnp.logical_and(hit, first >= 0), j, second)
            first = jnp.where(jnp.logical_and(hit, first < 0), j, first)
        for r, src in ((0, first), (1, second)):
            start = jnp.maximum(src, 0) * BLOCK
            keep = jnp.where(src >= 0, jnp.float32(1.0), jnp.float32(0.0))
            block = x_ref[:, pl.ds(start, BLOCK)].astype(jnp.float32) * keep
            slots[s, :, pl.ds(r * BLOCK, BLOCK)] = block.astype(jnp.bfloat16)
        return carry

    for copy in inputs:
        copy.wait()
    lax.fori_loop(0, AHEAD, fill, 0)

    pl.semaphore_wait(barrier, nblk * 2 + NY - 1 + jnp.where(bp == c, 0, 1))

    my_rows = pl.ds(pl.multiple_of(c * panel, panel), panel)
    my_cols = pl.ds(pl.multiple_of(bm * W, W), W)

    def st_copy(i, d):
        s = target(i)
        dst = a_buf.at[y, my_rows, my_cols] if d == 0 else o_buf.at[my_rows, my_cols]
        return pltpu.make_async_remote_copy(
            src_ref=slots.at[s],
            dst_ref=dst,
            send_sem=st_send.at[d, i],
            recv_sem=st_recv.at[d, bm, c],
            device_id=(s, tm_of(y, h if d == 0 else 1 - h, bp)),
            device_id_type=MESH,
        )

    @pl.when(bp == c)
    def _():
        pltpu.make_async_copy(
            slots.at[b], a_buf.at[y, my_rows, my_cols], st_recv.at[0, bm, c]
        ).start()

    @pl.when(bp != c)
    def _():
        st_copy(0, 0).start()

    def send_one(i, carry):
        @pl.when(i + AHEAD - 1 < nblk)
        def _():
            fill(i + AHEAD - 1, 0)

        @pl.when(i < nblk)
        def _():
            st_copy(i, 0).start()

        @pl.when(i >= LAG)
        def _():
            st_copy(i - LAG, 1).start()
        return carry

    lax.fori_loop(1, nblk + LAG, send_one, 0)

    def clear(u, carry):
        acc_s[u] = jnp.zeros((half, half), jnp.float32)
        acc_x[u] = jnp.zeros((half, half), jnp.float32)
        return carry

    lax.fori_loop(0, NY, clear, 0)
    sum_acc[...] = jnp.zeros(sum_acc.shape, jnp.float32)

    def st_wait(d, m, q):
        rows = pl.ds(q * panel, panel)
        cols = pl.ds(pl.multiple_of(m * W, W), W)
        dst = a_buf.at[y, rows, cols] if d == 0 else o_buf.at[rows, cols]
        pltpu.make_async_remote_copy(
            src_ref=slots.at[0], dst_ref=dst, send_sem=st_send.at[d, 0], recv_sem=st_recv.at[d, m, q],
            device_id=other, device_id_type=MESH,
        ).wait_recv()

    whole = pl.ds(0, half)

    def y_copy(m, way, src_y, q, to_y):
        rows = pl.ds(q * panel, panel)
        cols = pl.ds(pl.multiple_of(m * W, W), W)
        return pltpu.make_async_remote_copy(
            src_ref=a_buf.at[src_y, rows, cols],
            dst_ref=a_buf.at[src_y, rows, cols],
            send_sem=y_send.at[m, way],
            recv_sem=y_recv.at[m, way],
            device_id=(b, tm_of(to_y, h, c)),
            device_id_type=MESH,
        )

    def source(j):
        k = (2 * j + (b + c) % 2) * STRIDE % nblk
        return ((b + nblk - k) % nblk) // 2

    ones = jnp.ones((8, W), jnp.bfloat16)

    first = pl.ds(0, half - BLOCK)
    last = pl.ds(half - BLOCK, BLOCK)

    def split(u, v):
        return jnp.logical_and(u < CUT, v >= CUT)

    def near(u, v):
        return jnp.logical_and(u <= v, jnp.logical_or(u >= CUT, v < CUT))

    def job_sum(m, u):
        cols = pl.ds(pl.multiple_of(m * W, W), W)
        sum_acc[u] += dot_t(ones, a_buf[u, :, cols])

    def job_cross(m, u):
        cols = pl.ds(pl.multiple_of(m * W, W), W)

        @pl.when(near(u, y))
        def _():
            acc_x[u] += dot_t(a_buf[u, :, cols], o_buf[:, cols])

        @pl.when(split(u, y))
        def _():
            acc_x[u, :, first] += dot_t(a_buf[u, :, cols], o_buf[first, cols])

        @pl.when(split(y, u))
        def _():
            acc_x[u, :, 0:BLOCK] += dot_t(o_buf[:, cols], a_buf[u, last, cols])

    def job_same(m, u):
        cols = pl.ds(pl.multiple_of(m * W, W), W)

        @pl.when(u >= y)
        def _():
            acc_s[u] += dot_t(a_buf[y, :, cols], a_buf[u, :, cols])

    def job(m, u):
        job_sum(m, u)
        job_cross(m, u)
        job_same(m, u)

    def neighbour(r):
        return (y + r + r // 2) % NY

    def other_sum(m):
        cols = pl.ds(pl.multiple_of(m * W, W), W)
        sum_acc[NY] += dot_t(ones, o_buf[:, cols])

    def await_near(m):
        y_copy(m, 1, down, 1, y).wait_recv()
        y_copy(m, 2, up, 0, y).wait_recv()
        for q in range(2):
            st_wait(1, m, q)

    def multiply_near(m):
        other_sum(m)

        def one(r, carry):
            job(m, neighbour(r))
            return carry

        lax.fori_loop(0, 3, one, 0)

    def multiply_far(m):
        y_copy(m, 4, far, 0, y).wait_recv()
        y_copy(m, 5, far, 1, y).wait_recv()
        job(m, far)

    def step(j, carry):
        @pl.when(j < nsrc)
        def _():
            m = source(j)
            st_wait(0, m, 0)
            y_copy(m, 0, y, 0, up).start()
            st_wait(0, m, 1)
            y_copy(m, 3, y, 1, down).start()
            y_copy(m, 1, y, 1, up).start()
            y_copy(m, 2, y, 0, down).start()

        @pl.when(j >= 1)
        def _():
            m = source(j - 1)
            y_copy(m, 0, down, 0, y).wait_recv()
            y_copy(m, 4, down, 0, up).start()
            y_copy(m, 3, up, 1, y).wait_recv()
            y_copy(m, 5, up, 1, down).start()

        @pl.when(j >= 2)
        def _():
            multiply_far(source(j - 2))

        @pl.when(jnp.logical_and(j >= 1, j < nsrc))
        def _():
            m = source(j - 1)
            await_near(m)
            multiply_near(m)
        return carry

    lax.fori_loop(0, nsrc + 1, step, 0)

    theirs = pl.ds(pl.multiple_of((1 - c) * panel, panel), panel)
    mine = pl.ds(pl.multiple_of(c * panel, panel), panel)

    end = source(nsrc - 1)
    head = a_buf[y, 0:16, :].astype(jnp.float32)
    lane = lax.broadcasted_iota(jnp.int32, head.shape, 1)
    row = lax.broadcasted_iota(jnp.int32, head.shape, 0)
    mark = jnp.where(jnp.logical_and(lane % BLOCK == 0, row == 0), head, 0.0)
    filled = jnp.sum(jnp.where(mark > 0.0, 1.0, 0.0))
    srow = lax.broadcasted_iota(jnp.int32, (8, half), 0)

    def s_copy(u):
        return pltpu.make_async_remote_copy(
            src_ref=s_mine.at[u], dst_ref=s_oth.at[u], send_sem=s_send.at[u], recv_sem=s_recv.at[u],
            device_id=other, device_id_type=MESH,
        )

    def share_sum(u):
        s_mine[u] = jnp.where(srow == 1, filled, sum_acc[u])
        s_copy(u).start()

    def take_sum(u):
        s_copy(u).wait_recv()
        total = s_mine[u] + s_oth[u]
        s_tot[u] = total
        s_col[u] = total.T

    def c_copy(kind, u):
        src, dst = (acc_s, rs) if kind == 0 else (acc_x, rx)
        return pltpu.make_async_remote_copy(
            src_ref=src.at[u, theirs, :], dst_ref=dst.at[u],
            send_sem=c_send.at[kind, u], recv_sem=c_recv.at[kind, u],
            device_id=other, device_id_type=MESH,
        )

    def t_copy(yy, u):
        cols = pl.ds(pl.multiple_of(yy * 2 * half + (1 - h) * half, half), half)
        return pltpu.make_async_remote_copy(
            src_ref=tsum.at[u], dst_ref=out_ref.at[:, cols],
            send_sem=t_send.at[u], recv_sem=t_recv.at[yy],
            device_id=(b, tm_of(u, h, c)), device_id_type=MESH,
        )

    def t_split(yy, u):
        start = yy * 2 * half + (1 - h) * half
        cols = pl.ds(pl.multiple_of(start, BLOCK), half - BLOCK)
        return pltpu.make_async_remote_copy(
            src_ref=tsum.at[u, :, first], dst_ref=out_ref.at[:, cols],
            send_sem=t_send.at[u], recv_sem=t_recv.at[yy],
            device_id=(b, tm_of(u, h, c)), device_id_type=MESH,
        )

    def z_copy(v, hh):
        start = v * 2 * half + hh * half + half - BLOCK
        cols = pl.ds(pl.multiple_of(start, BLOCK), BLOCK)
        return pltpu.make_async_remote_copy(
            src_ref=tsum.at[v, :, 0:BLOCK], dst_ref=out_ref.at[:, cols],
            send_sem=t_send.at[v], recv_sem=z_recv.at[v],
            device_id=(b, tm_of(y, 1 - h, c)), device_id_type=MESH,
        )

    def share_same(u):
        @pl.when(u >= y)
        def _():
            c_copy(0, u).start()

    def scaled(g, u_row, u_col, cols):
        si = s_col[u_row, mine, 0:1]
        sj = s_tot[u_col, 0:1, cols]
        return g * (s_tot[NY, 1:2, 0:1] * BLOCK) / (si * sj)

    def back(u):
        c_copy(1, u).wait_recv()

        @pl.when(jnp.logical_and(u < y, near(u, y)))
        def _():
            tsum[u] = scaled(acc_x[u, mine, :] + rx[u], u, NY, whole)
            t_copy(y, u).start()

        @pl.when(split(u, y))
        def _():
            tsum[u, :, first] = scaled(acc_x[u, mine, first] + rx[u, :, first], u, NY, first)
            t_split(y, u).start()

        @pl.when(split(y, u))
        def _():
            tsum[u, :, 0:BLOCK] = scaled(
                acc_x[u, mine, 0:BLOCK] + rx[u, :, 0:BLOCK], NY, u, last
            )
            z_copy(u, h).start()

    await_near(end)
    other_sum(end)
    share_sum(NY)

    def near_sum(r, carry):
        job_sum(end, neighbour(r))
        share_sum(neighbour(r))
        return carry

    def near_cross(r, carry):
        job_cross(end, neighbour(r))
        c_copy(1, neighbour(r)).start()
        return carry

    def near_same(r, carry):
        job_same(end, neighbour(r))
        share_same(neighbour(r))
        return carry

    def near_take(r, carry):
        take_sum(neighbour(r))
        return carry

    def near_back(r, carry):
        back(neighbour(r))
        return carry

    lax.fori_loop(0, 3, near_sum, 0)
    lax.fori_loop(0, 3, near_cross, 0)
    lax.fori_loop(0, 3, near_same, 0)
    take_sum(NY)
    lax.fori_loop(0, 3, near_take, 0)
    lax.fori_loop(0, 3, near_back, 0)
    y_copy(end, 4, far, 0, y).wait_recv()
    y_copy(end, 5, far, 1, y).wait_recv()
    job_sum(end, far)
    share_sum(far)
    job_cross(end, far)
    c_copy(1, far).start()
    job_same(end, far)
    share_same(far)
    take_sum(far)
    back(far)

    tile = lax.broadcasted_iota(jnp.int32, (panel, half), 1)

    def place(u, carry):
        same_cols = pl.ds(pl.multiple_of(u * 2 * half + h * half, half), half)
        cross_cols = pl.ds(pl.multiple_of(u * 2 * half + (1 - h) * half, half), half)

        @pl.when(u < y)
        def _():
            out_ref[:, same_cols] = jnp.zeros((panel, half), jnp.float32)
            out_ref[:, cross_cols] = jnp.zeros((panel, half), jnp.float32)

        @pl.when(u >= y)
        def _():
            c_copy(0, u).wait_recv()
            g = scaled(acc_s[u, mine, :] + rs[u], y, u, whole)
            first_tile = u * 4 + h * 2
            tiles = first_tile + jnp.where(tile >= panel, 1, 0)
            out_ref[:, same_cols] = jnp.where(tiles >= t, g, 0.0)

        @pl.when(u == y)
        def _():
            g = scaled(acc_x[u, mine, :] + rx[u], y, NY, whole)
            first_tile = u * 4 + (1 - h) * 2
            tiles = first_tile + jnp.where(tile >= panel, 1, 0)
            out_ref[:, cross_cols] = jnp.where(tiles >= t, g, 0.0)
        return carry

    lax.fori_loop(0, NY, place, 0)

    @pl.when(bp != c)
    def _():
        st_copy(0, 0).wait_send()

    def drain_one(i, carry):
        @pl.when(i >= 1)
        def _():
            st_copy(i, 0).wait_send()
        st_copy(i, 1).wait_send()
        return carry

    lax.fori_loop(0, nblk, drain_one, 0)

    def drain_y(m, carry):
        y_copy(m, 0, y, 0, up).wait_send()
        y_copy(m, 1, y, 1, up).wait_send()
        y_copy(m, 2, y, 0, down).wait_send()
        y_copy(m, 3, y, 1, down).wait_send()
        y_copy(m, 4, down, 0, up).wait_send()
        y_copy(m, 5, up, 1, down).wait_send()
        return carry

    lax.fori_loop(0, nsrc, drain_y, 0)

    def arrive(u, carry):
        @pl.when(jnp.logical_and(u > y, near(y, u)))
        def _():
            t_copy(u, y).wait_recv()

        @pl.when(split(y, u))
        def _():
            t_split(u, y).wait_recv()
            z_copy(u, 1 - h).wait_recv()
        return carry

    lax.fori_loop(0, NY, arrive, 0)

    def drain_c(u, carry):
        c_copy(1, u).wait_send()

        @pl.when(u >= y)
        def _():
            c_copy(0, u).wait_send()

        @pl.when(jnp.logical_and(u < y, near(u, y)))
        def _():
            t_copy(y, u).wait_send()

        @pl.when(split(u, y))
        def _():
            t_split(y, u).wait_send()

        @pl.when(split(y, u))
        def _():
            z_copy(u, h).wait_send()
        return carry

    lax.fori_loop(0, NY, drain_c, 0)
    for u in range(NY + 1):
        s_copy(u).wait_send()


def on_device(intensity, block_cycle, cycle_order):
    panel = intensity.shape[0]
    nblk = cycle_order.shape[0]
    nsrc = nblk // 2
    half = 2 * panel
    frames = panel * lax.axis_size("tm")
    vmem = pl.BlockSpec(memory_space=pltpu.VMEM)
    hbm = pl.BlockSpec(memory_space=pltpu.HBM)
    dma = pltpu.SemaphoreType.DMA
    twotime = pl.pallas_call(
        main_kernel,
        out_shape=jax.ShapeDtypeStruct((panel, frames), jnp.float32),
        in_specs=[hbm, hbm, hbm],
        out_specs=vmem,
        scratch_shapes=[
            pltpu.SMEM(block_cycle.shape, jnp.int32),
            pltpu.SMEM(cycle_order.shape, jnp.int32),
            pltpu.VMEM(intensity.shape, jnp.bfloat16),
            pltpu.VMEM((nblk, panel, W), jnp.bfloat16),
            pltpu.VMEM((NY, half, nsrc * W), jnp.bfloat16),
            pltpu.VMEM((half, nsrc * W), jnp.bfloat16),
            pltpu.VMEM((NY, half, half), jnp.float32),
            pltpu.VMEM((NY, half, half), jnp.float32),
            pltpu.VMEM((NY, panel, half), jnp.float32),
            pltpu.VMEM((NY, panel, half), jnp.float32),
            pltpu.VMEM((NY, panel, half), jnp.float32),
            pltpu.VMEM((NY + 1, 8, half), jnp.float32),
            pltpu.VMEM((NY + 1, 8, half), jnp.float32),
            pltpu.VMEM((NY + 1, 8, half), jnp.float32),
            pltpu.VMEM((NY + 1, 8, half), jnp.float32),
            pltpu.VMEM((NY + 1, half, 8), jnp.float32),
            dma((2, nblk)), dma((2, nsrc, 2)),
            dma((nsrc, 6)), dma((nsrc, 6)),
            dma((2, NY)), dma((2, NY)),
            dma((NY,)), dma((NY,)), dma((NY,)),
            dma((NY + 1,)), dma((NY + 1,)), dma((3,)),
        ],
        compiler_params=pltpu.CompilerParams(
            collective_id=0, has_side_effects=True, vmem_limit_bytes=32 << 20
        ),
        name="exchange",
    )(*(pltpu.with_memory_space_constraint(a, pltpu.HBM) for a in (block_cycle, cycle_order, intensity)))
    return twotime.reshape(1, panel, frames)


def solution(mesh):
    placed = (P("tm", "blk"), P("blk"), P())
    return jax.shard_map(
        on_device, mesh=mesh, in_specs=placed, out_specs=P("blk", "tm", None), check_vma=False
    )
```

```python
import jax
import jax.numpy as jnp
from jax import lax
from jax.experimental import pallas as pl
from jax.experimental.pallas import tpu as pltpu
from jax.sharding import PartitionSpec as P

BLOCK = 128
MESH = pl.DeviceIdType.MESH
NY = 4
W = 2 * BLOCK
STRIDE = 7
LAG = 1
AHEAD = 2
CUT = 2


def dot_t(a, b):
    return lax.dot_general(a, b, (((1,), (1,)), ((), ())), preferred_element_type=jnp.float32)


def main_kernel(
    bc_hbm, order_hbm, x_hbm, out_ref,
    bc_ref, order_ref, x_ref, slots, a_buf, o_buf, acc_s, acc_x, rs, rx, tsum, sum_acc, s_mine, s_oth, s_tot, s_col,
    st_send, st_recv, y_send, y_recv, c_send, c_recv, t_send, t_recv, z_recv, s_send, s_recv, in_sem,
):
    nblk, panel, _ = slots.shape
    nsrc = nblk // 2
    b = lax.axis_index("blk")
    t = lax.axis_index("tm")
    c = t % 2
    h = (t // 2) % 2
    y = t // 4
    bp = b % 2
    bm = b // 2
    half = 2 * panel
    up = (y + 1) % NY
    down = (y + NY - 1) % NY
    far = (y + 2) % NY

    def tm_of(yy, hh, cc):
        return (yy * 2 + hh) * 2 + cc

    other = (b, tm_of(y, h, 1 - c))

    inputs = [
        pltpu.make_async_copy(src, dst, in_sem.at[i])
        for i, (src, dst) in enumerate(((bc_hbm, bc_ref), (order_hbm, order_ref), (x_hbm, x_ref)))
    ]
    for copy in inputs:
        copy.start()

    barrier = pltpu.get_barrier_semaphore()

    def greet(k, carry):
        s = (bm + k) % nsrc * 2 + c
        for j in range(4):
            pl.semaphore_signal(barrier, inc=1, device_id=(s, y * 4 + j), device_id_type=MESH)
        return carry

    @pl.when(bp == c)
    def _():
        for j in range(1, 4):
            to = (b, y * 4 + (t + j) % 4)
            pl.semaphore_signal(barrier, inc=1, device_id=to, device_id_type=MESH)

    @pl.when(bp != c)
    def _():
        greet(0, 0)
        pl.semaphore_signal(barrier, inc=1, device_id=other, device_id_type=MESH)
        to = (b, tm_of(y, 1 - h, c))
        pl.semaphore_signal(barrier, inc=1, device_id=to, device_id_type=MESH)

    lax.fori_loop(1, nsrc, greet, 0)
    for r in range(1, NY):
        pl.semaphore_signal(
            barrier, inc=1, device_id=(b, tm_of((y + r) % NY, h, c)), device_id_type=MESH
        )

    blk_dev = x_ref.shape[1] // BLOCK

    def target(i):
        return (b + i * STRIDE) % nblk

    def fill(i, carry):
        s = target(i)
        cyc = order_ref[s]
        first = jnp.int32(-1)
        second = jnp.int32(-1)
        for j in range(blk_dev):
            hit = bc_ref[j] == cyc
            second = jnp.where(jnp.logical_and(hit, first >= 0), j, second)
            first = jnp.where(jnp.logical_and(hit, first < 0), j, first)
        for r, src in ((0, first), (1, second)):
            start = jnp.maximum(src, 0) * BLOCK
            keep = jnp.where(src >= 0, jnp.float32(1.0), jnp.float32(0.0))
            block = x_ref[:, pl.ds(start, BLOCK)].astype(jnp.float32) * keep
            slots[s, :, pl.ds(r * BLOCK, BLOCK)] = block.astype(jnp.bfloat16)
        return carry

    for copy in inputs:
        copy.wait()
    lax.fori_loop(0, AHEAD, fill, 0)

    pl.semaphore_wait(barrier, nblk * 2 + NY - 1 + jnp.where(bp == c, 0, 1))

    my_rows = pl.ds(pl.multiple_of(c * panel, panel), panel)
    my_cols = pl.ds(pl.multiple_of(bm * W, W), W)

    def st_copy(i, d):
        s = target(i)
        dst = a_buf.at[y, my_rows, my_cols] if d == 0 else o_buf.at[my_rows, my_cols]
        return pltpu.make_async_remote_copy(
            src_ref=slots.at[s],
            dst_ref=dst,
            send_sem=st_send.at[d, i],
            recv_sem=st_recv.at[d, bm, c],
            device_id=(s, tm_of(y, h if d == 0 else 1 - h, bp)),
            device_id_type=MESH,
        )

    @pl.when(bp == c)
    def _():
        pltpu.make_async_copy(
            slots.at[b], a_buf.at[y, my_rows, my_cols], st_recv.at[0, bm, c]
        ).start()

    @pl.when(bp != c)
    def _():
        st_copy(0, 0).start()

    def send_one(i, carry):
        @pl.when(i + AHEAD - 1 < nblk)
        def _():
            fill(i + AHEAD - 1, 0)

        @pl.when(i < nblk)
        def _():
            st_copy(i, 0).start()

        @pl.when(i >= LAG)
        def _():
            st_copy(i - LAG, 1).start()
        return carry

    lax.fori_loop(1, nblk + LAG, send_one, 0)

    def clear(u, carry):
        acc_s[u] = jnp.zeros((half, half), jnp.float32)
        acc_x[u] = jnp.zeros((half, half), jnp.float32)
        return carry

    lax.fori_loop(0, NY, clear, 0)
    sum_acc[...] = jnp.zeros(sum_acc.shape, jnp.float32)

    def st_wait(d, m, q):
        rows = pl.ds(q * panel, panel)
        cols = pl.ds(pl.multiple_of(m * W, W), W)
        dst = a_buf.at[y, rows, cols] if d == 0 else o_buf.at[rows, cols]
        pltpu.make_async_remote_copy(
            src_ref=slots.at[0], dst_ref=dst, send_sem=st_send.at[d, 0], recv_sem=st_recv.at[d, m, q],
            device_id=other, device_id_type=MESH,
        ).wait_recv()

    whole = pl.ds(0, half)

    def y_copy(m, way, src_y, q, to_y):
        rows = pl.ds(q * panel, panel)
        cols = pl.ds(pl.multiple_of(m * W, W), W)
        return pltpu.make_async_remote_copy(
            src_ref=a_buf.at[src_y, rows, cols],
            dst_ref=a_buf.at[src_y, rows, cols],
            send_sem=y_send.at[m, way],
            recv_sem=y_recv.at[m, way],
            device_id=(b, tm_of(to_y, h, c)),
            device_id_type=MESH,
        )

    def source(j):
        k = (2 * j + (b + c) % 2) * STRIDE % nblk
        return ((b + nblk - k) % nblk) // 2

    ones = jnp.ones((8, W), jnp.bfloat16)

    first = pl.ds(0, half - BLOCK)
    last = pl.ds(half - BLOCK, BLOCK)

    def split(u, v):
        return jnp.logical_and(u < CUT, v >= CUT)

    def near(u, v):
        return jnp.logical_and(u <= v, jnp.logical_or(u >= CUT, v < CUT))

    def job_sum(m, u):
        cols = pl.ds(pl.multiple_of(m * W, W), W)
        sum_acc[u] += dot_t(ones, a_buf[u, :, cols])

    def job_cross(m, u):
        cols = pl.ds(pl.multiple_of(m * W, W), W)

        @pl.when(near(u, y))
        def _():
            acc_x[u] += dot_t(a_buf[u, :, cols], o_buf[:, cols])

        @pl.when(split(u, y))
        def _():
            acc_x[u, :, first] += dot_t(a_buf[u, :, cols], o_buf[first, cols])

        @pl.when(split(y, u))
        def _():
            acc_x[u, :, 0:BLOCK] += dot_t(o_buf[:, cols], a_buf[u, last, cols])

    def job_same(m, u):
        cols = pl.ds(pl.multiple_of(m * W, W), W)

        @pl.when(u >= y)
        def _():
            acc_s[u] += dot_t(a_buf[y, :, cols], a_buf[u, :, cols])

    def job(m, u):
        job_sum(m, u)
        job_cross(m, u)
        job_same(m, u)

    def neighbour(r):
        return (y + 1 + r + (r + 1) // 2) % NY

    def other_sum(m):
        cols = pl.ds(pl.multiple_of(m * W, W), W)
        sum_acc[NY] += dot_t(ones, o_buf[:, cols])

    def await_near(m):
        y_copy(m, 1, down, 1, y).wait_recv()
        y_copy(m, 2, up, 0, y).wait_recv()
        for q in range(2):
            st_wait(1, m, q)

    def multiply_near(m):
        other_sum(m)

        def one(r, carry):
            job(m, neighbour(r))
            return carry

        lax.fori_loop(0, 3, one, 0)

    def multiply_far(m):
        y_copy(m, 4, far, 0, y).wait_recv()
        y_copy(m, 5, far, 1, y).wait_recv()
        job(m, far)

    def step(j, carry):
        @pl.when(j < nsrc)
        def _():
            m = source(j)
            st_wait(0, m, 0)
            y_copy(m, 0, y, 0, up).start()
            st_wait(0, m, 1)
            y_copy(m, 3, y, 1, down).start()
            y_copy(m, 1, y, 1, up).start()
            y_copy(m, 2, y, 0, down).start()

        @pl.when(j >= 1)
        def _():
            m = source(j - 1)
            y_copy(m, 0, down, 0, y).wait_recv()
            y_copy(m, 4, down, 0, up).start()
            y_copy(m, 3, up, 1, y).wait_recv()
            y_copy(m, 5, up, 1, down).start()

        @pl.when(j >= 2)
        def _():
            multiply_far(source(j - 2))

        @pl.when(jnp.logical_and(j >= 1, j < nsrc))
        def _():
            m = source(j - 1)
            await_near(m)
            multiply_near(m)
        return carry

    lax.fori_loop(0, nsrc + 1, step, 0)

    theirs = pl.ds(pl.multiple_of((1 - c) * panel, panel), panel)
    mine = pl.ds(pl.multiple_of(c * panel, panel), panel)

    end = source(nsrc - 1)
    head = a_buf[y, 0:16, :].astype(jnp.float32)
    lane = lax.broadcasted_iota(jnp.int32, head.shape, 1)
    row = lax.broadcasted_iota(jnp.int32, head.shape, 0)
    mark = jnp.where(jnp.logical_and(lane % BLOCK == 0, row == 0), head, 0.0)
    filled = jnp.sum(jnp.where(mark > 0.0, 1.0, 0.0))
    srow = lax.broadcasted_iota(jnp.int32, (8, half), 0)

    def s_copy(u):
        return pltpu.make_async_remote_copy(
            src_ref=s_mine.at[u], dst_ref=s_oth.at[u], send_sem=s_send.at[u], recv_sem=s_recv.at[u],
            device_id=other, device_id_type=MESH,
        )

    def share_sum(u):
        s_mine[u] = jnp.where(srow == 1, filled, sum_acc[u])
        s_copy(u).start()

    def take_sum(u):
        s_copy(u).wait_recv()
        total = s_mine[u] + s_oth[u]
        s_tot[u] = total
        s_col[u] = total.T

    def c_copy(kind, u):
        src, dst = (acc_s, rs) if kind == 0 else (acc_x, rx)
        return pltpu.make_async_remote_copy(
            src_ref=src.at[u, theirs, :], dst_ref=dst.at[u],
            send_sem=c_send.at[kind, u], recv_sem=c_recv.at[kind, u],
            device_id=other, device_id_type=MESH,
        )

    def t_copy(yy, u):
        cols = pl.ds(pl.multiple_of(yy * 2 * half + (1 - h) * half, half), half)
        return pltpu.make_async_remote_copy(
            src_ref=tsum.at[u], dst_ref=out_ref.at[:, cols],
            send_sem=t_send.at[u], recv_sem=t_recv.at[yy],
            device_id=(b, tm_of(u, h, c)), device_id_type=MESH,
        )

    def t_split(yy, u):
        start = yy * 2 * half + (1 - h) * half
        cols = pl.ds(pl.multiple_of(start, BLOCK), half - BLOCK)
        return pltpu.make_async_remote_copy(
            src_ref=tsum.at[u, :, first], dst_ref=out_ref.at[:, cols],
            send_sem=t_send.at[u], recv_sem=t_recv.at[yy],
            device_id=(b, tm_of(u, h, c)), device_id_type=MESH,
        )

    def z_copy(v, hh):
        start = v * 2 * half + hh * half + half - BLOCK
        cols = pl.ds(pl.multiple_of(start, BLOCK), BLOCK)
        return pltpu.make_async_remote_copy(
            src_ref=tsum.at[v, :, 0:BLOCK], dst_ref=out_ref.at[:, cols],
            send_sem=t_send.at[v], recv_sem=z_recv.at[v],
            device_id=(b, tm_of(y, 1 - h, c)), device_id_type=MESH,
        )

    def share_same(u):
        @pl.when(u >= y)
        def _():
            c_copy(0, u).start()

    def scaled(g, u_row, u_col, cols):
        si = s_col[u_row, mine, 0:1]
        sj = s_tot[u_col, 0:1, cols]
        return g * (s_tot[NY, 1:2, 0:1] * BLOCK) / (si * sj)

    def back(u):
        c_copy(1, u).wait_recv()

        @pl.when(jnp.logical_and(u < y, near(u, y)))
        def _():
            tsum[u] = scaled(acc_x[u, mine, :] + rx[u], u, NY, whole)
            t_copy(y, u).start()

        @pl.when(split(u, y))
        def _():
            tsum[u, :, first] = scaled(acc_x[u, mine, first] + rx[u, :, first], u, NY, first)
            t_split(y, u).start()

        @pl.when(split(y, u))
        def _():
            tsum[u, :, 0:BLOCK] = scaled(
                acc_x[u, mine, 0:BLOCK] + rx[u, :, 0:BLOCK], NY, u, last
            )
            z_copy(u, h).start()

    await_near(end)
    other_sum(end)
    share_sum(NY)

    def near_sum(r, carry):
        job_sum(end, neighbour(r))
        share_sum(neighbour(r))
        return carry

    def near_cross(r, carry):
        job_cross(end, neighbour(r))
        c_copy(1, neighbour(r)).start()
        return carry

    def near_same(r, carry):
        job_same(end, neighbour(r))
        share_same(neighbour(r))
        return carry

    def near_take(r, carry):
        take_sum(neighbour(r))
        return carry

    def near_back(r, carry):
        back(neighbour(r))
        return carry

    lax.fori_loop(0, 3, near_sum, 0)
    lax.fori_loop(0, 3, near_cross, 0)
    lax.fori_loop(0, 3, near_same, 0)
    take_sum(NY)
    lax.fori_loop(0, 3, near_take, 0)
    lax.fori_loop(0, 3, near_back, 0)
    y_copy(end, 4, far, 0, y).wait_recv()
    y_copy(end, 5, far, 1, y).wait_recv()
    job_sum(end, far)
    share_sum(far)
    job_cross(end, far)
    c_copy(1, far).start()
    job_same(end, far)
    share_same(far)
    take_sum(far)
    back(far)

    tile = lax.broadcasted_iota(jnp.int32, (panel, half), 1)

    def place(u, carry):
        same_cols = pl.ds(pl.multiple_of(u * 2 * half + h * half, half), half)
        cross_cols = pl.ds(pl.multiple_of(u * 2 * half + (1 - h) * half, half), half)

        @pl.when(u < y)
        def _():
            out_ref[:, same_cols] = jnp.zeros((panel, half), jnp.float32)
            out_ref[:, cross_cols] = jnp.zeros((panel, half), jnp.float32)

        @pl.when(u >= y)
        def _():
            c_copy(0, u).wait_recv()
            g = scaled(acc_s[u, mine, :] + rs[u], y, u, whole)
            first_tile = u * 4 + h * 2
            tiles = first_tile + jnp.where(tile >= panel, 1, 0)
            out_ref[:, same_cols] = jnp.where(tiles >= t, g, 0.0)

        @pl.when(u == y)
        def _():
            g = scaled(acc_x[u, mine, :] + rx[u], y, NY, whole)
            first_tile = u * 4 + (1 - h) * 2
            tiles = first_tile + jnp.where(tile >= panel, 1, 0)
            out_ref[:, cross_cols] = jnp.where(tiles >= t, g, 0.0)
        return carry

    lax.fori_loop(0, NY, place, 0)

    @pl.when(bp != c)
    def _():
        st_copy(0, 0).wait_send()

    def drain_one(i, carry):
        @pl.when(i >= 1)
        def _():
            st_copy(i, 0).wait_send()
        st_copy(i, 1).wait_send()
        return carry

    lax.fori_loop(0, nblk, drain_one, 0)

    def drain_y(m, carry):
        y_copy(m, 0, y, 0, up).wait_send()
        y_copy(m, 1, y, 1, up).wait_send()
        y_copy(m, 2, y, 0, down).wait_send()
        y_copy(m, 3, y, 1, down).wait_send()
        y_copy(m, 4, down, 0, up).wait_send()
        y_copy(m, 5, up, 1, down).wait_send()
        return carry

    lax.fori_loop(0, nsrc, drain_y, 0)

    def arrive(u, carry):
        @pl.when(jnp.logical_and(u > y, near(y, u)))
        def _():
            t_copy(u, y).wait_recv()

        @pl.when(split(y, u))
        def _():
            t_split(u, y).wait_recv()
            z_copy(u, 1 - h).wait_recv()
        return carry

    lax.fori_loop(0, NY, arrive, 0)

    def drain_c(u, carry):
        c_copy(1, u).wait_send()

        @pl.when(u >= y)
        def _():
            c_copy(0, u).wait_send()

        @pl.when(jnp.logical_and(u < y, near(u, y)))
        def _():
            t_copy(y, u).wait_send()

        @pl.when(split(u, y))
        def _():
            t_split(y, u).wait_send()

        @pl.when(split(y, u))
        def _():
            z_copy(u, h).wait_send()
        return carry

    lax.fori_loop(0, NY, drain_c, 0)
    for u in range(NY + 1):
        s_copy(u).wait_send()


def on_device(intensity, block_cycle, cycle_order):
    panel = intensity.shape[0]
    nblk = cycle_order.shape[0]
    nsrc = nblk // 2
    half = 2 * panel
    frames = panel * lax.axis_size("tm")
    vmem = pl.BlockSpec(memory_space=pltpu.VMEM)
    hbm = pl.BlockSpec(memory_space=pltpu.HBM)
    dma = pltpu.SemaphoreType.DMA
    twotime = pl.pallas_call(
        main_kernel,
        out_shape=jax.ShapeDtypeStruct((panel, frames), jnp.float32),
        in_specs=[hbm, hbm, hbm],
        out_specs=vmem,
        scratch_shapes=[
            pltpu.SMEM(block_cycle.shape, jnp.int32),
            pltpu.SMEM(cycle_order.shape, jnp.int32),
            pltpu.VMEM(intensity.shape, jnp.bfloat16),
            pltpu.VMEM((nblk, panel, W), jnp.bfloat16),
            pltpu.VMEM((NY, half, nsrc * W), jnp.bfloat16),
            pltpu.VMEM((half, nsrc * W), jnp.bfloat16),
            pltpu.VMEM((NY, half, half), jnp.float32),
            pltpu.VMEM((NY, half, half), jnp.float32),
            pltpu.VMEM((NY, panel, half), jnp.float32),
            pltpu.VMEM((NY, panel, half), jnp.float32),
            pltpu.VMEM((NY, panel, half), jnp.float32),
            pltpu.VMEM((NY + 1, 8, half), jnp.float32),
            pltpu.VMEM((NY + 1, 8, half), jnp.float32),
            pltpu.VMEM((NY + 1, 8, half), jnp.float32),
            pltpu.VMEM((NY + 1, 8, half), jnp.float32),
            pltpu.VMEM((NY + 1, half, 8), jnp.float32),
            dma((2, nblk)), dma((2, nsrc, 2)),
            dma((nsrc, 6)), dma((nsrc, 6)),
            dma((2, NY)), dma((2, NY)),
            dma((NY,)), dma((NY,)), dma((NY,)),
            dma((NY + 1,)), dma((NY + 1,)), dma((3,)),
        ],
        compiler_params=pltpu.CompilerParams(
            collective_id=0, has_side_effects=True, vmem_limit_bytes=32 << 20
        ),
        name="exchange",
    )(*(pltpu.with_memory_space_constraint(a, pltpu.HBM) for a in (block_cycle, cycle_order, intensity)))
    return twotime.reshape(1, panel, frames)


def solution(mesh):
    placed = (P("tm", "blk"), P("blk"), P())
    return jax.shard_map(
        on_device, mesh=mesh, in_specs=placed, out_specs=P("blk", "tm", None), check_vma=False
    )
```
